32 devices in a mesh: rep: 4 (over y, x), shard: 8 (over z, core).
Axes of the slice: x: 2, y: 2, z: 4, core: 2. Of those that a mesh axis runs over, the one named last changes fastest.
Arguments:
- tokens: bfloat16 [8192, 1024], P(('rep', 'shard')), may hold values from -6 to 6
- choices: int32 [8192, 8], P(('rep', 'shard')), may hold values from 0 to 31, all different within a row; in each aligned block of 256 rows (0 to 255, 256 to 511, ...) at most 96 rows name the same one
- cont_lengths: int32 [4, 2], P('rep'), may hold values from 1 to 768, 1024 in all within a row
- norm_attn: bfloat16 [1024], P('shard'), may hold values from 0.5 to 1.5
- w_qkv: bfloat16 [1024, 2048], P('shard'), may hold values from -0.1875 to 0.1875
- w_out: bfloat16 [1024, 1024], P('shard'), may hold values from -1.5 to 1.5
- norm_ffn: bfloat16 [1024], P('shard'), may hold values from 0.5 to 1.5
- w_router: bfloat16 [1024, 32], P('shard'), may hold values from -0.25 to 0.25
- w_gate_up: bfloat16 [32, 1024, 1024], P('shard'), may hold values from -0.1875 to 0.1875
- w_down: bfloat16 [32, 512, 1024], P('shard'), may hold values from -0.25 to 0.25
- cotangent: bfloat16 [8192, 1024], P(('rep', 'shard')), may hold values from -6 to 6
Outputs:
- output: bfloat16 [8192, 1024], P(('rep', 'shard'))
- d_tokens: float32 [8192, 1024], P(('rep', 'shard'))
- grad_norm_attn: float32 [1024], P('shard')
- grad_qkv: float32 [1024, 2048], P('shard')
- grad_out: float32 [1024, 1024], P('shard')
- grad_norm_ffn: float32 [1024], P('shard')
- grad_router: float32 [1024, 32], P('shard')
- grad_gate_up: float32 [32, 1024, 1024], P('shard')
- grad_down: float32 [32, 512, 1024], P('shard')
The draws below stay inside these ranges and needn't reach their ends.
Inputs may be any that keep to these rules, and one draw needn't show every extreme that they name: `choices`: in the rows of one device (aligned blocks of 256 rows) no expert is named by more than 96 rows, a bound that some block reaches; a row names 8 different experts. `cont_lengths`: each row holds the 2 continuation lengths of one group; they sum to 1024 and none is longer than 768.
All inputs are finite; a program needn't handle non-finite values.
Results may differ from the reference program's by a relative error of at most 0.02.
Values may be sent and summed in bfloat16 or wider, within the bound.
A program may use at most 192 MiB of HBM per device.

```python
import math
import jax
import jax.numpy as jnp
import numpy as np
from jax import lax

D = 1024
HEADS = 16
KV_HEADS = 8
HEAD = 64
EXPERTS = 32
FF = 512
TOPK = 8
TOK_DEV = 256
GROUP = 2048
GROUPS = 4
TOKENS = 8192
PROMPT = 1024
CONT = 2
CMOST = 768
CAP = 96
N_SHARD = 8


def levels(stream_key, dims, shards, low, top_value):
    gain, own = 1.0, jax.random.fold_in(stream_key, 6)
    for dim, parts in shards:
        draws = jnp.exp(jax.random.uniform(jax.random.fold_in(own, dim), (parts,), jnp.float32, low / len(shards), top_value / len(shards)))
        gain = gain * jnp.repeat(draws, dims[dim] // parts).reshape([-1 if axis == dim else 1 for axis in range(len(dims))])
    return gain


def length_profile(number_of, total, reach, skew):
    loads = [(1 << 20) // math.isqrt(grade ** skew) + 1 for grade in range(2, number_of + 1)]
    spare, counts = total - reach - (number_of - 1), [1] * (number_of - 1)
    while spare > 0:
        candidates = [i for i in range(number_of - 1) if counts[i] < reach]
        mass, budget = sum([loads[i] for i in candidates]), spare
        for i in candidates:
            extra = min(reach - counts[i], max(1, budget * loads[i] // mass), spare)
            counts[i] = counts[i] + extra
            spare = spare - extra
    return np.array([reach] + counts)


def uneven(own_key, amount, total, most, lean):
    if amount == 2:
        one = jax.random.randint(own_key, (), max(1, total - most), min(most, total - 1) + 1)
        return jnp.stack([one, total - one])
    sizes = jnp.asarray(length_profile(amount, total, most, lean), jnp.int32)
    couples = (amount - 1) // 2
    donor, receiver = sizes[1:1 + 2 * couples:2], sizes[2:2 + 2 * couples:2]
    room = jnp.minimum(donor - 1, most - receiver)
    shifted = jax.random.randint(jax.random.fold_in(own_key, 1), (couples,), 0, 1 << 20) % (room + 1)
    sizes = sizes.at[1:1 + 2 * couples:2].set(donor - shifted).at[2:2 + 2 * couples:2].set(receiver + shifted)
    return sizes[jax.random.permutation(jax.random.fold_in(own_key, 2), amount)]


def assign_block(stream_key, own, number, rows, number_of, top, bound, lean):
    ranking = jax.random.permutation(stream_key, number_of)
    crowded, common = shares(number_of, rows * top, bound, lean, True), shares(number_of, rows * top, bound, lean, False)
    places = jnp.arange(number_of)

    def named(sizes, rotation):
        used = int((sizes > 0).sum())
        fixed = max(1, used // 4)
        shifted = fixed + (places - fixed + rotation * (used - fixed)) % max(1, number_of - fixed)
        return jnp.zeros((number_of,), jnp.int32).at[ranking[jnp.where(places < fixed, places, shifted)]].set(jnp.asarray(sizes, jnp.int32))

    sizes = jnp.where(number % 4 == 0, named(crowded, number // 4), named(common, number - number // 4 - 1))
    mixed = jax.random.permutation(jax.random.fold_in(own, 3), number_of)
    source_of, receiver = mixed[0:number_of // 2 * 2:2], mixed[1:number_of // 2 * 2:2]
    margin = jnp.minimum(sizes[source_of] - 1, bound - sizes[receiver]) // 2
    margin = jnp.where((source_of == ranking[0]) | (receiver == ranking[0]) | (sizes[receiver] == 0), 0, jnp.maximum(margin, 0))
    shifted = jax.random.randint(jax.random.fold_in(own, 4), (number_of // 2,), 0, 1 << 20) % (margin + 1)
    sizes = sizes.at[source_of].add(-shifted).at[receiver].add(shifted)
    items = jnp.searchsorted(jnp.cumsum(sizes), jnp.arange(rows * top), side="right").astype(jnp.int32)
    grid = items.reshape(top, rows).T
    grid = grid[jax.random.permutation(jax.random.fold_in(own, 1), rows)]
    rotation = jax.random.randint(jax.random.fold_in(own, 2), (rows, 1), 0, top)
    return jnp.take_along_axis(grid, (jnp.arange(top)[None, :] + rotation) % top, axis=1)


def shares(amount, total, most, skew, full):
    loads = [(1 << 20) // math.isqrt(rank ** skew) + 1 for rank in range(1, amount + 1)]
    largest = most if full else min(most, max(-(-total // amount), total * loads[0] // sum(loads)))
    least = 1 if total - largest >= amount - 1 else 0
    given, spare = [largest] + [least] * (amount - 1), total - largest - least * (amount - 1)
    while spare > 0:
        movable = [i for i in range(1, amount) if given[i] < largest] or [i for i in range(1, amount) if given[i] < most]
        mass, left = sum([loads[i] for i in movable]), spare
        for i in movable:
            addition = min(most - given[i], max(1, left * loads[i] // mass), spare)
            given[i] = given[i] + addition
            spare = spare - addition
    return np.array(given)


def noise(own_key, shape, width, bound, cuts=(), kind=jnp.bfloat16):
    result = width * jax.random.normal(own_key, shape, jnp.float32)
    if cuts:
        result = result * levels(own_key, shape, cuts, -0.22, 0.18)
    return jnp.clip(result, -bound, bound).astype(kind)


def setup_inputs(seed: int = 0) -> dict:
    seeds = jax.random.split(jax.random.key(seed), 12)
    tokens = noise(seeds[0], (TOKENS, D), 1.0, 6.0, ((0, 32),))
    choices_keys = jax.random.split(jax.random.fold_in(seeds[1], 1), TOKENS // TOK_DEV)
    choices_turns = jax.random.permutation(jax.random.fold_in(seeds[1], 3), TOKENS // TOK_DEV)
    choices = jax.vmap(lambda own, number: assign_block(jax.random.fold_in(seeds[1], 2), own, number, TOK_DEV, EXPERTS, TOPK, CAP, 1))(choices_keys, choices_turns).reshape((TOKENS, TOPK))
    cont_lengths = jax.vmap(lambda own: uneven(own, CONT, PROMPT, CMOST, 2))(jax.random.split(seeds[2], GROUPS)).reshape((GROUPS, CONT)).astype(jnp.int32)
    norm_attn = jnp.clip(1.0 + 0.1 * jax.random.normal(seeds[3], (D,), jnp.float32), 0.5, 1.5).astype(jnp.bfloat16)
    w_qkv = noise(seeds[4], (D, (HEADS + 2 * KV_HEADS) * HEAD), D ** -0.5, 0.1875, ((0, 8),))
    w_out = noise(seeds[5], (HEADS * HEAD, D), (max(1, HEADS * HEAD * 16 // PROMPT)) ** -0.5, 1.5, ((0, 8),))
    norm_ffn = jnp.clip(1.0 + 0.1 * jax.random.normal(seeds[6], (D,), jnp.float32), 0.5, 1.5).astype(jnp.bfloat16)
    w_router = noise(seeds[7], (D, EXPERTS), (0.5 * D ** -0.5), 0.25, ((0, 8),))
    w_gate_up = noise(seeds[8], (EXPERTS, D, 2 * FF), D ** -0.5, 0.1875, ((0, 8),))
    w_down = noise(seeds[9], (EXPERTS, FF, D), FF ** -0.5, 0.25, ((0, 8),))
    cotangent = noise(seeds[10], (TOKENS, D), 1.0, 6.0, ((0, 32),))
    return {"tokens": tokens, "choices": choices, "cont_lengths": cont_lengths, "norm_attn": norm_attn, "w_qkv": w_qkv, "w_out": w_out, "norm_ffn": norm_ffn, "w_router": w_router, "w_gate_up": w_gate_up, "w_down": w_down, "cotangent": cotangent}


EPSILON = 1e-06
HIGHEST = lax.Precision.HIGHEST

@jax.custom_vjp
def low(v):
    return lax.optimization_barrier(v.astype(jnp.bfloat16)).astype(jnp.float32)

@jax.custom_vjp
def low_back(v):
    return v

def low_keep(v):
    return (low(v), None)

def low_pass(kept, grad):
    return (grad,)

def back_keep(v):
    return (v, None)

def back_low(kept, grad):
    return (low(grad),)
low.defvjp(low_keep, low_pass)
low_back.defvjp(back_keep, back_low)

def layout(lengths, tok_index, prompt_len):
    starts = prompt_len + jnp.cumsum(lengths) - lengths
    passed = tok_index[:, None] >= starts[None, :]
    segment = lax.optimization_barrier(jnp.sum(passed.astype(jnp.int32), axis=1))
    seg_start = lax.optimization_barrier(jnp.max(jnp.where(passed, starts[None, :], 0), axis=1))
    position = jnp.where(segment > 0, tok_index - seg_start + prompt_len, tok_index)
    return (segment.astype(jnp.int32), position.astype(jnp.int32))

def rotary(field_rows, position, direction):
    half_width = field_rows.shape[-1] // 2
    freq_table = 10000.0 ** (-jnp.arange(half_width, dtype=jnp.float32) / half_width)
    angle_table = direction * position.astype(jnp.float32)[:, None] * freq_table[None, :]
    cosine = jnp.cos(angle_table)[:, None, :]
    sine_part = jnp.sin(angle_table)[:, None, :]
    first_half = field_rows[..., :half_width]
    second_half = field_rows[..., half_width:]
    return jnp.concatenate([first_half * cosine - second_half * sine_part, second_half * cosine + first_half * sine_part], axis=-1)

def group_forward(tokens_f, choices, lengths, weights):
    norm_attn, w_qkv, w_out, norm_ffn, w_router, w_gate_up, w_down = weights
    row_count = tokens_f.shape[0]
    prompt_len = row_count // 2
    tok_index = jnp.arange(row_count, dtype=jnp.int32)
    segment, position = layout(lengths, tok_index, prompt_len)
    normed = tokens_f * lax.rsqrt(lax.optimization_barrier(jnp.mean(tokens_f * tokens_f, axis=1, keepdims=True)) + EPSILON)
    first_in = low(normed * norm_attn)
    qkv_rows = low_back(jnp.dot(first_in, w_qkv, precision=HIGHEST))
    query_width = HEADS * HEAD
    key_width = KV_HEADS * HEAD
    repeat_count = HEADS // KV_HEADS
    queries = low(rotary(qkv_rows[:, :query_width].reshape(row_count, HEADS, HEAD), position, 1.0))
    queries = queries.reshape(row_count, KV_HEADS, repeat_count, HEAD)
    key_rot = low(rotary(qkv_rows[:, query_width:query_width + key_width].reshape(row_count, KV_HEADS, HEAD), position, 1.0))
    values = low(qkv_rows[:, query_width + key_width:].reshape(row_count, KV_HEADS, HEAD))
    query_block = min(512, row_count)
    blocks = row_count // query_block

    def attend(block_piece):
        block_queries, block_index, block_segment = block_piece
        scores = low_back(jnp.einsum('qgrd,kgd->grqk', block_queries, key_rot, precision=HIGHEST) * HEAD ** (-0.5))
        allowed = (tok_index[None, :] <= block_index[:, None]) & ((segment[None, :] == 0) | (segment[None, :] == block_segment[:, None]))
        scores = jnp.where(allowed, scores, -1e+30)
        prob_low = low(jax.nn.softmax(scores, axis=-1))
        return jnp.einsum('grqk,kgd->qgrd', prob_low, values, precision=HIGHEST)
    mixed_heads = lax.map(jax.checkpoint(attend), (queries.reshape(blocks, query_block, KV_HEADS, repeat_count, HEAD), tok_index.reshape(blocks, query_block), segment.reshape(blocks, query_block)))
    mixed_heads = low_back(low(mixed_heads.reshape(row_count, query_width)))
    residual = tokens_f + low_back(jnp.dot(mixed_heads, w_out, precision=HIGHEST))
    normed_two = residual * lax.rsqrt(lax.optimization_barrier(jnp.mean(residual * residual, axis=1, keepdims=True)) + EPSILON)
    second_in = low(normed_two * norm_ffn)
    logits = jnp.dot(second_in, w_router, precision=HIGHEST)
    chosen = jnp.take_along_axis(logits, choices, axis=1)
    gate_weights = jax.nn.softmax(chosen, axis=-1)
    pair_count = row_count * TOPK
    flat_choice = choices.reshape(-1)
    onehot = (flat_choice[:, None] == jnp.arange(EXPERTS, dtype=jnp.int32)[None, :]).astype(jnp.int32)
    slot_rank = lax.optimization_barrier(jnp.sum((jnp.cumsum(onehot, axis=0) - onehot) * onehot, axis=1))
    group_cap = CAP * N_SHARD
    slot_place = (flat_choice * group_cap + slot_rank).astype(jnp.int32)
    slot_pair = jnp.full((EXPERTS * group_cap,), pair_count, jnp.int32).at[slot_place].set(jnp.arange(pair_count, dtype=jnp.int32))
    padded = jnp.concatenate([second_in, jnp.zeros((1, D), second_in.dtype)], axis=0)
    slot_rows = low_back(padded[slot_pair // TOPK].reshape(EXPERTS, group_cap, D))
    gate_up = low_back(jnp.einsum('ecd,edf->ecf', slot_rows, w_gate_up, precision=HIGHEST))
    hidden = low(jax.nn.silu(gate_up[..., :FF]) * gate_up[..., FF:])
    expert_out = low_back(low(jnp.einsum('ecf,efd->ecd', hidden, w_down, precision=HIGHEST)))
    pair_out = expert_out.reshape(EXPERTS * group_cap, D)[slot_place].reshape(row_count, TOPK, D)
    return residual + lax.optimization_barrier(jnp.sum(gate_weights[:, :, None] * pair_out, axis=1))

def forward(tokens_f, choices, lengths, weights):

    def one_group(state_acc, group_piece):
        return (state_acc, jax.checkpoint(group_forward)(group_piece[0], group_piece[1], group_piece[2], weights))
    unused, group_outs = lax.scan(one_group, jnp.zeros((), jnp.float32), (tokens_f.reshape(GROUPS, GROUP, D), choices.reshape(GROUPS, GROUP, TOPK), lengths))
    return group_outs.reshape(TOKENS, D)

def reference(tokens, choices, cont_lengths, norm_attn, w_qkv, w_out, norm_ffn, w_router, w_gate_up, w_down, cotangent):
    weights_f = tuple((weight.astype(jnp.float32) for weight in (norm_attn, w_qkv, w_out, norm_ffn, w_router, w_gate_up, w_down)))

    def full_pass(tokens_f, *weight_list):
        return forward(tokens_f, choices, cont_lengths, weight_list)
    output, pull_back = jax.vjp(full_pass, tokens.astype(jnp.float32), *weights_f)
    gradients = pull_back(cotangent.astype(jnp.float32))
    return (output.astype(jnp.bfloat16), gradients[0], gradients[1], gradients[2], gradients[3], gradients[4], gradients[5], gradients[6], gradients[7])
```

```python
import jax
import jax.numpy as jnp
from jax import lax
from jax.sharding import PartitionSpec as P

HEADS = 16
KV_HEADS = 8
HEAD = 64
EXPERTS = 32
FF = 512
TOPK = 8
CAP = 96


EPSILON = 1e-06


def layout(lengths, tok_index, prompt_len):
    order = jnp.arange(lengths.shape[0])
    starts = prompt_len + jnp.sum(jnp.where(order[None, :] < order[:, None], lengths[None, :], 0), axis=1)
    passed = tok_index[:, None] >= starts[None, :]
    segment = jnp.sum(passed.astype(jnp.int32), axis=1)
    seg_start = jnp.max(jnp.where(passed, starts[None, :], 0), axis=1)
    position = jnp.where(segment > 0, tok_index - seg_start + prompt_len, tok_index)
    return (segment, position)


def rotary(field_rows, position, direction):
    half_width = field_rows.shape[-1] // 2
    freq_table = 10000.0 ** (-jnp.arange(half_width, dtype=jnp.float32) / half_width)
    angle_table = direction * position.astype(jnp.float32)[:, None] * freq_table[None, :]
    cosine = jnp.cos(angle_table)[:, None, :]
    sine_part = jnp.sin(angle_table)[:, None, :]
    first_half = field_rows[..., :half_width]
    second_half = field_rows[..., half_width:]
    return jnp.concatenate(
        [
            first_half * cosine - second_half * sine_part,
            second_half * cosine + first_half * sine_part,
        ],
        axis=-1,
    )


def block_scores(queries, query_index, query_segment, key_rot, key_index, key_segment):
    scores = jnp.einsum(
        "qgrd,kgd->grqk", queries, key_rot, preferred_element_type=jnp.float32
    ) * queries.shape[-1] ** (-0.5)
    allowed = (key_index[None, :] <= query_index[:, None]) & (
        (key_segment[None, :] == 0) | (key_segment[None, :] == query_segment[:, None])
    )
    return (jnp.where(allowed, scores, -1e30), allowed)


def gate_table(logits, named):
    masked = jnp.where(named, logits, -1e30)
    weight = jnp.where(named, jnp.exp(masked - jnp.max(masked, axis=1, keepdims=True)), 0.0)
    return weight / jnp.sum(weight, axis=1, keepdims=True)


def on_device(
    tokens,
    choices,
    cont_lengths,
    norm_attn,
    w_qkv,
    w_out,
    norm_ffn,
    w_router,
    w_gate_up,
    w_down,
    cotangent,
):
    row_count = tokens.shape[0]
    model_width = tokens.shape[1]
    shard_count = lax.axis_size("shard")
    group_len = row_count * shard_count
    prompt_len = group_len // 2
    lengths_row = cont_lengths[0]
    tok_index = lax.axis_index("shard") * row_count + jnp.arange(row_count, dtype=jnp.int32)
    segment, position = layout(lengths_row, tok_index, prompt_len)
    gain_attn, full_qkv, full_out, gain_ffn, full_router = (
        lax.all_gather(norm_attn, "shard", axis=0, tiled=True),
        lax.all_gather(w_qkv, "shard", axis=0, tiled=True),
        lax.all_gather(w_out, "shard", axis=0, tiled=True),
        lax.all_gather(norm_ffn, "shard", axis=0, tiled=True),
        lax.all_gather(w_router, "shard", axis=0, tiled=True),
    )
    gain_attn = gain_attn.astype(jnp.float32)
    gain_ffn = gain_ffn.astype(jnp.float32)
    tokens_f = tokens.astype(jnp.float32)
    inv_one = lax.rsqrt(jnp.mean(tokens_f * tokens_f, axis=1, keepdims=True) + EPSILON)
    normed_one = tokens_f * inv_one
    first_in = (normed_one * gain_attn).astype(jnp.bfloat16)
    qkv_rows = jnp.dot(first_in, full_qkv, preferred_element_type=jnp.float32)
    query_width = HEADS * HEAD
    key_width = KV_HEADS * HEAD
    repeat_count = HEADS // KV_HEADS
    score_scale = HEAD ** (-0.5)
    queries = (
        rotary(qkv_rows[:, :query_width].reshape(row_count, HEADS, HEAD), position, 1.0)
        .astype(jnp.bfloat16)
        .reshape(row_count, KV_HEADS, repeat_count, HEAD)
    )
    key_rot = rotary(
        qkv_rows[:, query_width : query_width + key_width].reshape(row_count, KV_HEADS, HEAD),
        position,
        1.0,
    ).astype(jnp.bfloat16)
    values = (
        qkv_rows[:, query_width + key_width :]
        .astype(jnp.bfloat16)
        .reshape(row_count, KV_HEADS, HEAD)
    )
    all_keys, all_values = (
        lax.all_gather(key_rot, "shard", axis=0, tiled=True),
        lax.all_gather(values, "shard", axis=0, tiled=True),
    )
    key_block = min(512, prompt_len)
    blocks = group_len // key_block
    group_index = jnp.arange(group_len, dtype=jnp.int32)
    group_segment, group_position = layout(lengths_row, group_index, prompt_len)
    key_stack = (
        all_keys.reshape(blocks, key_block, KV_HEADS, HEAD),
        all_values.reshape(blocks, key_block, KV_HEADS, HEAD),
        group_index.reshape(blocks, key_block),
        group_segment.reshape(blocks, key_block),
    )
    stat_shape = (KV_HEADS, repeat_count, row_count)

    def stats_step(state_acc, key_piece):
        run_max, run_sum = state_acc
        scores, allowed = block_scores(
            queries, tok_index, segment, key_piece[0], key_piece[2], key_piece[3]
        )
        new_max = jnp.maximum(run_max, jnp.max(scores, axis=-1))
        run_sum = run_sum * jnp.exp(run_max - new_max) + jnp.sum(
            jnp.where(allowed, jnp.exp(scores - new_max[..., None]), 0.0), axis=-1
        )
        return ((new_max, run_sum), None)

    (run_max, run_sum), unused = lax.scan(
        stats_step,
        (jnp.full(stat_shape, -1e30, jnp.float32), jnp.zeros(stat_shape, jnp.float32)),
        key_stack,
    )
    log_total = run_max + jnp.log(run_sum)

    def prob_block(key_piece):
        scores, allowed = block_scores(
            queries, tok_index, segment, key_piece[0], key_piece[2], key_piece[3]
        )
        return jnp.where(allowed, jnp.exp(scores - log_total[..., None]), 0.0)

    def mix_step(total_mix, key_piece):
        prob_f32 = prob_block(key_piece)
        return (
            total_mix
            + jnp.einsum(
                "grqk,kgd->qgrd",
                prob_f32.astype(jnp.bfloat16),
                key_piece[1],
                preferred_element_type=jnp.float32,
            ),
            None,
        )

    mix_f32, unused = lax.scan(
        mix_step, jnp.zeros((row_count, KV_HEADS, repeat_count, HEAD), jnp.float32), key_stack
    )
    mixed_heads = mix_f32.reshape(row_count, query_width).astype(jnp.bfloat16)
    residual = tokens_f + jnp.dot(mixed_heads, full_out, preferred_element_type=jnp.float32)
    inv_two = lax.rsqrt(jnp.mean(residual * residual, axis=1, keepdims=True) + EPSILON)
    normed_two = residual * inv_two
    second_in = (normed_two * gain_ffn).astype(jnp.bfloat16)
    logits = jnp.dot(second_in, full_router, preferred_element_type=jnp.float32)
    local_experts = w_down.shape[0]
    expert_ids = jnp.arange(EXPERTS, dtype=jnp.int32)
    local_ids = lax.axis_index("shard") * local_experts + jnp.arange(local_experts, dtype=jnp.int32)
    group_in = lax.all_gather(second_in, "shard", axis=0, tiled=True)
    group_cot = lax.all_gather(cotangent, "shard", axis=0, tiled=True)
    group_choice = lax.all_gather(choices, "shard", axis=0, tiled=True)
    named = jnp.any(choices[:, :, None] == expert_ids[None, None, :], axis=1)
    gates = gate_table(logits, named)
    group_named = jnp.any(group_choice[:, :, None] == expert_ids[None, None, :], axis=1)
    group_logits = jnp.dot(group_in, full_router, preferred_element_type=jnp.float32)
    group_gates = gate_table(group_logits, group_named)
    own = (expert_ids[:, None] == local_ids[None, :]).astype(jnp.float32)
    own_gates = jnp.sum(group_gates[:, :, None] * own[None], axis=1).reshape(
        shard_count, row_count, local_experts
    )
    own_named = jnp.sum(group_named.astype(jnp.float32)[:, :, None] * own[None], axis=1).reshape(
        shard_count, row_count, local_experts
    )
    earlier = (
        jnp.arange(row_count)[:, None] > jnp.arange(row_count)[None, :]
    ).astype(jnp.bfloat16)
    rank = jnp.einsum(
        "st,nte->nse", earlier, own_named.astype(jnp.bfloat16), preferred_element_type=jnp.float32
    )
    rank = jnp.where(own_named > 0, rank, -1.0)
    hit = rank.transpose(0, 2, 1)[:, :, None, :] == jnp.arange(CAP, dtype=jnp.float32)[
        None, None, :, None
    ]
    pick = hit.astype(jnp.bfloat16)
    slot_gates = jnp.sum(
        jnp.where(hit, own_gates.transpose(0, 2, 1)[:, :, None, :], 0.0), axis=3
    ).transpose(1, 0, 2)
    group_in = group_in.reshape(shard_count, row_count, model_width)
    group_cot = group_cot.reshape(shard_count, row_count, model_width)
    slots = shard_count * CAP
    received = (
        jnp.einsum("nest,ntd->ensd", pick, group_in, preferred_element_type=jnp.float32)
        .astype(jnp.bfloat16)
        .reshape(local_experts, slots, model_width)
    )
    slot_cot = jnp.einsum(
        "nest,ntd->ensd", pick, group_cot, preferred_element_type=jnp.float32
    ).reshape(local_experts, slots, model_width)
    slot_gates = slot_gates.reshape(local_experts, slots)
    d_received = (slot_cot * slot_gates[:, :, None]).astype(jnp.bfloat16)
    gate_up = jnp.einsum("ecd,edf->ecf", received, w_gate_up, preferred_element_type=jnp.float32)
    gate_part = gate_up[..., :FF]
    up_part = gate_up[..., FF:]
    sigmoid_gate = jax.nn.sigmoid(gate_part)
    silu_gate = gate_part * sigmoid_gate
    hidden = (silu_gate * up_part).astype(jnp.bfloat16)
    expert_out = jnp.einsum("ecf,efd->ecd", hidden, w_down, preferred_element_type=jnp.float32)
    scaled_out = (expert_out * slot_gates[:, :, None]).astype(jnp.bfloat16)
    slot_d_gates = jnp.sum(expert_out * slot_cot, axis=2)
    out_terms = jnp.einsum(
        "nest,ensd->ntd",
        pick,
        scaled_out.reshape(local_experts, shard_count, CAP, model_width),
        preferred_element_type=jnp.float32,
    ).reshape(group_len, model_width)
    pair_sum = lax.psum_scatter(
        out_terms.astype(jnp.bfloat16), "shard", scatter_dimension=0, tiled=True
    ).astype(jnp.float32)
    output = (residual + pair_sum).astype(jnp.bfloat16)
    grad_in = cotangent.astype(jnp.float32)
    own_d_gates = jnp.sum(
        jnp.where(
            hit, slot_d_gates.reshape(local_experts, shard_count, CAP).transpose(1, 0, 2)[..., None], 0.0
        ),
        axis=2,
    ).transpose(0, 2, 1)
    d_gates = lax.all_to_all(
        own_d_gates.reshape(group_len, local_experts), "shard", split_axis=0, concat_axis=1, tiled=True
    )
    d_hidden = jnp.einsum("ecd,efd->ecf", d_received, w_down, preferred_element_type=jnp.float32)
    d_gate_up = jnp.concatenate(
        [
            d_hidden * up_part * sigmoid_gate * (1.0 + gate_part * (1.0 - sigmoid_gate)),
            d_hidden * silu_gate,
        ],
        axis=-1,
    ).astype(jnp.bfloat16)
    grad_down = jnp.einsum("ecf,ecd->efd", hidden, d_received, preferred_element_type=jnp.float32)
    grad_gate_up = jnp.einsum("ecd,ecf->edf", received, d_gate_up, preferred_element_type=jnp.float32)
    d_slots = jnp.einsum(
        "ecf,edf->ecd", d_gate_up, w_gate_up, preferred_element_type=jnp.float32
    ).astype(jnp.bfloat16)
    d_terms = jnp.einsum(
        "nest,ensd->ntd",
        pick,
        d_slots.reshape(local_experts, shard_count, CAP, model_width),
        preferred_element_type=jnp.float32,
    ).reshape(group_len, model_width)
    d_second = lax.psum_scatter(
        d_terms.astype(jnp.bfloat16), "shard", scatter_dimension=0, tiled=True
    ).astype(jnp.float32)
    d_logits = gates * (d_gates - jnp.sum(gates * d_gates, axis=1, keepdims=True))
    d_second = d_second + jnp.dot(
        d_logits, full_router.astype(jnp.float32).T, precision=lax.Precision.HIGHEST
    )
    grad_router = jnp.dot(
        second_in.astype(jnp.float32).T, d_logits, precision=lax.Precision.HIGHEST
    )
    d_norm_two = d_second * gain_ffn
    grad_ffn = jnp.sum(d_second * normed_two, axis=0)
    d_residual = grad_in + inv_two * (
        d_norm_two - normed_two * jnp.mean(d_norm_two * normed_two, axis=1, keepdims=True)
    )
    d_attn = d_residual.astype(jnp.bfloat16)
    grad_out = jnp.dot(mixed_heads.T, d_attn, preferred_element_type=jnp.float32)
    d_mixed = (
        jnp.dot(d_attn, full_out.T, preferred_element_type=jnp.float32)
        .astype(jnp.bfloat16)
        .reshape(row_count, KV_HEADS, repeat_count, HEAD)
    )

    def delta_step(total_delta, key_piece):
        prob_f32 = prob_block(key_piece)
        d_prob = jnp.einsum(
            "qgrd,kgd->grqk", d_mixed, key_piece[1], preferred_element_type=jnp.float32
        )
        return (total_delta + jnp.sum(prob_f32 * d_prob, axis=-1), None)

    row_delta, unused = lax.scan(delta_step, jnp.zeros(stat_shape, jnp.float32), key_stack)

    def score_grad(key_piece):
        prob_f32 = prob_block(key_piece)
        d_prob = jnp.einsum(
            "qgrd,kgd->grqk", d_mixed, key_piece[1], preferred_element_type=jnp.float32
        )
        return (prob_f32, (prob_f32 * (d_prob - row_delta[..., None])).astype(jnp.bfloat16))

    query_zeros = jnp.zeros((row_count, KV_HEADS, repeat_count, HEAD), jnp.float32)

    def full_step(d_queries, key_piece):
        prob_f32, d_scores = score_grad(key_piece)
        d_queries = (
            d_queries
            + jnp.einsum(
                "grqk,kgd->qgrd", d_scores, key_piece[0], preferred_element_type=jnp.float32
            )
            * score_scale
        )
        key_term = (
            jnp.einsum("grqk,qgrd->kgd", d_scores, queries, preferred_element_type=jnp.float32)
            * score_scale
        )
        value_term = jnp.einsum(
            "grqk,qgrd->kgd",
            prob_f32.astype(jnp.bfloat16),
            d_mixed,
            preferred_element_type=jnp.float32,
        )
        return (d_queries, (key_term, value_term))

    d_queries, block_terms = lax.scan(full_step, query_zeros, key_stack)
    key_terms = block_terms[0].reshape(group_len, key_width)
    value_terms = block_terms[1].reshape(group_len, key_width)
    d_keys, d_values = (
        lax.psum_scatter(
            key_terms.astype(jnp.bfloat16), "shard", scatter_dimension=0, tiled=True
        ).astype(jnp.float32),
        lax.psum_scatter(
            value_terms.astype(jnp.bfloat16), "shard", scatter_dimension=0, tiled=True
        ).astype(jnp.float32),
    )
    d_keys = d_keys.reshape(row_count, KV_HEADS, HEAD)
    d_values = d_values.reshape(row_count, KV_HEADS, HEAD)
    d_query_rows = rotary(d_queries.reshape(row_count, HEADS, HEAD), position, -1.0).reshape(
        row_count, query_width
    )
    d_key_rows = rotary(d_keys, position, -1.0).reshape(row_count, key_width)
    d_qkv = jnp.concatenate(
        [d_query_rows, d_key_rows, d_values.reshape(row_count, key_width)], axis=1
    ).astype(jnp.bfloat16)
    grad_qkv = jnp.dot(first_in.T, d_qkv, preferred_element_type=jnp.float32)
    d_first = jnp.dot(d_qkv, full_qkv.T, preferred_element_type=jnp.float32)
    d_norm_one = d_first * gain_attn
    grad_attn = jnp.sum(d_first * normed_one, axis=0)
    d_tokens = d_residual + inv_one * (
        d_norm_one - normed_one * jnp.mean(d_norm_one * normed_one, axis=1, keepdims=True)
    )
    share_attn, share_qkv, share_out, share_ffn, share_router = (
        lax.psum_scatter(
            grad_attn.astype(jnp.bfloat16), "shard", scatter_dimension=0, tiled=True
        ).astype(jnp.float32),
        lax.psum_scatter(
            grad_qkv.astype(jnp.bfloat16), "shard", scatter_dimension=0, tiled=True
        ).astype(jnp.float32),
        lax.psum_scatter(
            grad_out.astype(jnp.bfloat16), "shard", scatter_dimension=0, tiled=True
        ).astype(jnp.float32),
        lax.psum_scatter(
            grad_ffn.astype(jnp.bfloat16), "shard", scatter_dimension=0, tiled=True
        ).astype(jnp.float32),
        lax.psum_scatter(
            grad_router.astype(jnp.bfloat16), "shard", scatter_dimension=0, tiled=True
        ).astype(jnp.float32),
    )
    share_attn, share_qkv, share_out, share_ffn, share_router, grad_gate_up, grad_down = (
        lax.psum(share_attn.astype(jnp.bfloat16), "rep").astype(jnp.float32),
        lax.psum(share_qkv.astype(jnp.bfloat16), "rep").astype(jnp.float32),
        lax.psum(share_out.astype(jnp.bfloat16), "rep").astype(jnp.float32),
        lax.psum(share_ffn.astype(jnp.bfloat16), "rep").astype(jnp.float32),
        lax.psum(share_router.astype(jnp.bfloat16), "rep").astype(jnp.float32),
        lax.psum(grad_gate_up.astype(jnp.bfloat16), "rep").astype(jnp.float32),
        lax.psum(grad_down.astype(jnp.bfloat16), "rep").astype(jnp.float32),
    )
    return (
        output,
        d_tokens,
        share_attn,
        share_qkv,
        share_out,
        share_ffn,
        share_router,
        grad_gate_up,
        grad_down,
    )


def solution(mesh):
    return jax.shard_map(
        on_device,
        mesh=mesh,
        in_specs=(
            P(("rep", "shard"), None),
            P(("rep", "shard"), None),
            P("rep", None),
            P("shard"),
            P("shard", None),
            P("shard", None),
            P("shard"),
            P("shard", None),
            P("shard", None, None),
            P("shard", None, None),
            P(("rep", "shard"), None),
        ),
        out_specs=(
            P(("rep", "shard"), None),
            P(("rep", "shard"), None),
            P("shard"),
            P("shard", None),
            P("shard", None),
            P("shard"),
            P("shard", None),
            P("shard", None, None),
            P("shard", None, None),
        ),
        check_vma=False,
    )
```

```python
import functools

import jax
import jax.numpy as jnp
from jax import lax
from jax.experimental import pallas as pl
from jax.experimental.pallas import tpu as pltpu
from jax.sharding import PartitionSpec as P

HEADS = 16
KV_HEADS = 8
HEAD = 64
EXPERTS = 32
FF = 512
TOPK = 8
CAP = 96
EPSILON = 1e-06


NEG = -1e30
KEYS = 512
LANES = 128


def swap_halves(x):
    lane = lax.broadcasted_iota(jnp.int32, x.shape, 1)
    return jnp.where(lane % HEAD < HEAD // 2, pltpu.roll(x, LANES - HEAD // 2, 1), pltpu.roll(x, HEAD // 2, 1))


def nt_dot(a, b):
    return lax.dot_general(a, b, (((1,), (1,)), ((), ())), preferred_element_type=jnp.float32)


def nn_dot(a, b):
    return jnp.dot(a, b, preferred_element_type=jnp.float32)


def split_kv(kv, low_lane):
    turned = pltpu.roll(kv, HEAD, 1)
    keys = (jnp.where(low_lane, kv, 0.0), jnp.where(low_lane, 0.0, turned))
    vals = (jnp.where(low_lane, turned, 0.0), jnp.where(low_lane, 0.0, kv))
    return keys, vals


def allowed_mask(lo, hi, query_base, start_row):
    key = lo + lax.broadcasted_iota(jnp.int32, (hi - lo, start_row.shape[1]), 0)
    query = query_base + lax.broadcasted_iota(jnp.int32, (hi - lo, start_row.shape[1]), 1)
    return (key <= query) & (key >= start_row)


def causal_chunks(block, prompt_blocks, span):
    free = min(block, prompt_blocks) * span
    end = (block + 1) * span
    cuts = [(k, min(k + KEYS, free), False) for k in range(0, free, KEYS)]
    return cuts + [(k, min(k + KEYS, end), True) for k in range(free, end, KEYS)]


def attend_forward_kernel(
    x_ref, gain_ref, w_ref, cos_ref, sin_ref, wout_ref, start_ref,
    part_ref, first_ref, q_ref, kv_ref, mix_ref, lse_ref,
    keys_s, vals_s, qt_s, s_s, p_s, acc_s,
):
    block = pl.program_id(0)
    span = q_ref.shape[0]
    blocks = keys_s.shape[1] // span
    x = x_ref[...].astype(jnp.float32)
    inv = lax.rsqrt(jnp.mean(x * x, axis=1, keepdims=True) + EPSILON)
    first = (x * inv * gain_ref[...]).astype(jnp.bfloat16)
    first_ref[...] = first
    qkv = nn_dot(first, w_ref[...])
    lane = lax.broadcasted_iota(jnp.int32, (span, LANES), 1)
    low_lane = lane < HEAD
    cosine, sine = cos_ref[...], sin_ref[...]
    q = qkv[:, :LANES]
    q = q * cosine + swap_halves(q) * sine
    kv = qkv[:, LANES:]
    kv = jnp.where(low_lane, kv * cosine + swap_halves(kv) * sine, kv)
    q_ref[...] = q.astype(jnp.bfloat16)
    kv_ref[...] = kv.astype(jnp.bfloat16)
    keys, unused = split_kv(kv, low_lane)
    here = pl.ds(pl.multiple_of(block * span, span), span)
    for h in range(2):
        keys_s[h, here] = keys[h].astype(jnp.bfloat16)
    vals_s[:, here] = jnp.transpose(kv)[HEAD:].astype(jnp.bfloat16)
    qt_s[...] = (jnp.transpose(q.astype(jnp.bfloat16).astype(jnp.float32)) * HEAD**-0.5).astype(jnp.bfloat16)

    def attend(i):
        chunks = causal_chunks(i, blocks // 2, span)
        end = (i + 1) * span
        q_t = qt_s[...]
        start_row = start_ref[...]
        for h in range(2):
            top = jnp.full((1, span), NEG, jnp.float32)
            for lo, hi, masked in chunks:
                s = nn_dot(keys_s[h, lo:hi], q_t)
                if masked:
                    s = jnp.where(allowed_mask(lo, hi, i * span, start_row), s, NEG)
                s_s[h, lo:hi] = s
                top = jnp.maximum(top, jnp.max(s, axis=0, keepdims=True))
            total = jnp.zeros((1, span), jnp.float32)
            for lo, hi, masked in chunks:
                p = jnp.exp(s_s[h, lo:hi] - top)
                total = total + jnp.sum(p, axis=0, keepdims=True)
                p_s[h, lo:hi] = p.astype(jnp.bfloat16)
            acc_s[h * HEAD : (h + 1) * HEAD] = nn_dot(vals_s[:, :end], p_s[h, :end]) / total
            lse_ref[h : h + 1, :] = top + jnp.log(total)

    for i in range(blocks):
        pl.when(block == i)(functools.partial(attend, i))
    mix_t = acc_s[...]
    mix_ref[...] = mix_t.astype(jnp.bfloat16)
    part_ref[...] = nn_dot(jnp.transpose(mix_t).astype(jnp.bfloat16), wout_ref[...]).astype(jnp.bfloat16)


def attend_backward_kernel(
    shards, da_ref, q_ref, kv_ref, mix_ref, lse_ref, start_ref, wout_ref, w_ref, first_ref, cos_ref, sin_ref,
    oparts_ref, residual_ref, dfirst_ref, gw_ref, gout_ref, out_ref,
    keys_s, vals_s, keyt_s, dk_s, dv_s, dq_s, dqt_s, gw_s, gout_s, p_s, ds_s, *scratch
):
    block = pl.program_id(0)
    span = q_ref.shape[0]
    blocks = keys_s.shape[1] // span
    fwd = Collect(shards // 2, oparts_ref, scratch)

    @pl.when(block == 0)
    def _():
        greet_shard(shards)
        fwd.start()

    lane = lax.broadcasted_iota(jnp.int32, (span, LANES), 1)
    low_lane = lane < HEAD

    @pl.when(block == 0)
    def _():
        def prepare(j, c):
            here = pl.ds(pl.multiple_of(j * span, span), span)
            kv = kv_ref[here].astype(jnp.float32)
            keys, vals = split_kv(kv, low_lane)
            for h in range(2):
                keys_s[h, here] = keys[h].astype(jnp.bfloat16)
                vals_s[h, here] = vals[h].astype(jnp.bfloat16)
            keyt_s[:, here] = jnp.transpose(kv)[:HEAD].astype(jnp.bfloat16)
            dk_s[here] = jnp.zeros((span, LANES), jnp.float32)
            dv_s[here] = jnp.zeros((span, LANES), jnp.float32)
            return c

        lax.fori_loop(0, blocks, prepare, 0)
        gout_s[...] = jnp.zeros_like(gout_s)
        gw_s[...] = jnp.zeros_like(gw_s)

    da = da_ref[...]
    dm_f = nt_dot(da, wout_ref[...])
    dm = dm_f.astype(jnp.bfloat16)
    dm_tf = jnp.transpose(dm.astype(jnp.float32))
    dm_t = dm_tf.astype(jnp.bfloat16)
    gout_s[...] += nn_dot(mix_ref[...], da)
    prod = mix_ref[...].astype(jnp.float32) * dm_tf
    delta = [jnp.sum(prod[h * HEAD : (h + 1) * HEAD], axis=0, keepdims=True) for h in range(2)]
    qs_f = q_ref[...].astype(jnp.float32) * HEAD**-0.5
    qs = qs_f.astype(jnp.bfloat16)
    q_t = jnp.transpose(qs_f).astype(jnp.bfloat16)

    def attend(i):
        chunks = causal_chunks(i, blocks // 2, span)
        end = (i + 1) * span
        start_row = start_ref[...]
        for h in range(2):
            for lo, hi, masked in chunks:
                s = nn_dot(keys_s[h, lo:hi], q_t)
                if masked:
                    s = jnp.where(allowed_mask(lo, hi, i * span, start_row), s, NEG)
                p = jnp.exp(s - lse_ref[h : h + 1, :])
                dp = nn_dot(vals_s[h, lo:hi], dm_t)
                p_s[h, lo:hi] = p.astype(jnp.bfloat16)
                ds_s[h, lo:hi] = (p * (dp - delta[h])).astype(jnp.bfloat16)
            dqt_s[h * HEAD : (h + 1) * HEAD] = nn_dot(keyt_s[:, :end], ds_s[h, :end])
        for lo, hi, masked in chunks:
            low_key = lax.broadcasted_iota(jnp.int32, (hi - lo, LANES), 1) < HEAD
            dv_s[lo:hi] += jnp.where(low_key, nn_dot(p_s[0, lo:hi], dm), nn_dot(p_s[1, lo:hi], dm))
            dk_s[lo:hi] += jnp.where(low_key, nn_dot(ds_s[0, lo:hi], qs), nn_dot(ds_s[1, lo:hi], qs))

    for i in range(blocks):
        pl.when(block == i)(functools.partial(attend, i))
    dq_s[block] = jnp.transpose(dqt_s[...]) * HEAD**-0.5
    hops = list(range(shards // 2 - 1, 0, -1))
    turns = {}
    for k, hop in enumerate(hops):
        turns.setdefault(0 if k == 0 else blocks - len(hops) + k, []).append(hop)
    for turn_block, some in turns.items():
        pl.when(block == turn_block)(functools.partial(fwd.carry, some))

    @pl.when(block == blocks - 1)
    def _():
        def finish(j, c):
            here = pl.ds(pl.multiple_of(j * span, span), span)
            dk = dk_s[here]
            dk = dk + pltpu.roll(dk, HEAD, 1)
            dv = dv_s[here]
            dv = dv + pltpu.roll(dv, HEAD, 1)
            cosine, sine = cos_ref[j], sin_ref[j]
            dkv = jnp.where(low_lane, dk * cosine - swap_halves(dk) * sine, dv).astype(jnp.bfloat16)
            dq = dq_s[j]
            dq = (dq * cosine - swap_halves(dq) * sine).astype(jnp.bfloat16)
            d_qkv = jnp.concatenate([dq, dkv], axis=1)
            d_qkv_t = jnp.transpose(d_qkv.astype(jnp.float32)).astype(jnp.bfloat16)
            gw_s[...] += nn_dot(d_qkv_t, first_ref[j])
            dfirst_ref[j] = nt_dot(d_qkv, w_ref[...]).astype(jnp.bfloat16)
            return c

        lax.fori_loop(0, blocks, finish, 0)
        shards, lines = gw_ref.shape[:2]
        cols = gw_s.shape[1] // shards
        for k in range(shards):
            for p in range(LANES // cols):
                gw_ref[k, :, p * cols : (p + 1) * cols] = gw_s[
                    p * lines : (p + 1) * lines, k * cols : (k + 1) * cols
                ].astype(jnp.bfloat16)
        for k in range(gout_s.shape[1] // LANES):
            gout_ref[k * LANES : (k + 1) * LANES] = gout_s[:, k * LANES : (k + 1) * LANES].astype(jnp.bfloat16)

        def finish_out(here, total):
            out_ref[here] = (residual_ref[here] + total).astype(jnp.bfloat16)

        for cut in range(2):
            fwd.finish(cut, finish_out)
        fwd.settle()


def attend_forward(x, gain, w, cosine, sine, w_out, start):
    total, width = x.shape
    span = 512 if total <= 2048 else 256
    blocks = total // span
    row = lambda cols: pl.BlockSpec((span, cols), lambda i: (i, 0))
    col = lambda rows: pl.BlockSpec((rows, span), lambda i: (0, i))
    fixed = lambda shape: pl.BlockSpec(shape, lambda i: tuple(0 for s in shape), pipeline_mode=pl.Buffered(1))
    shape = jax.ShapeDtypeStruct
    return pl.pallas_call(
        attend_forward_kernel,
        grid_spec=pltpu.PrefetchScalarGridSpec(
            num_scalar_prefetch=0,
            grid=(blocks,),
            in_specs=[row(width), fixed((1, width)), fixed(w.shape), row(LANES), row(LANES), fixed(w_out.shape), col(1)],
            out_specs=[row(width), row(width), row(LANES), row(LANES), col(LANES), col(2)],
            scratch_shapes=[
                pltpu.VMEM((2, total, LANES), jnp.bfloat16),
                pltpu.VMEM((HEAD, total), jnp.bfloat16),
                pltpu.VMEM((LANES, span), jnp.bfloat16),
                pltpu.VMEM((2, total, span), jnp.float32),
                pltpu.VMEM((2, total, span), jnp.bfloat16),
                pltpu.VMEM((LANES, span), jnp.float32),
            ],
        ),
        out_shape=[
            shape((total, width), jnp.bfloat16),
            shape((total, width), jnp.bfloat16),
            shape((total, LANES), jnp.bfloat16),
            shape((total, LANES), jnp.bfloat16),
            shape((LANES, total), jnp.bfloat16),
            shape((2, total), jnp.float32),
        ],
        compiler_params=pltpu.CompilerParams(dimension_semantics=("arbitrary",), vmem_limit_bytes=60 << 20),
        cost_estimate=cost(17),
        name="attend_forward",
    )(x, gain, w, cosine, sine, w_out, start)


def attend_backward(d_attn, q, kv, mix, lse, start, w_out, w, first, cosine, sine, o_parts, residual, shards):
    total, width = d_attn.shape
    span = 512 if total <= 2048 else 256
    blocks = total // span
    cols = w.shape[1]
    row = lambda cols: pl.BlockSpec((span, cols), lambda i: (i, 0))
    col = lambda rows: pl.BlockSpec((rows, span), lambda i: (0, i))
    fixed = lambda shape: pl.BlockSpec(shape, lambda i: tuple(0 for s in shape), pipeline_mode=pl.Buffered(1))
    shape = jax.ShapeDtypeStruct
    cut = lambda a: a.reshape(blocks, span, a.shape[1])
    return pl.pallas_call(
        functools.partial(attend_backward_kernel, shards),
        grid_spec=pltpu.PrefetchScalarGridSpec(
            num_scalar_prefetch=0,
            grid=(blocks,),
            in_specs=[
                row(width), row(LANES), fixed((total, LANES)), col(LANES), col(2), col(1),
                fixed(w_out.shape), fixed(w.shape), fixed((blocks, span, width)),
                fixed((blocks, span, LANES)), fixed((blocks, span, LANES)), ANY, fixed(residual.shape),
            ],
            out_specs=[fixed((blocks, span, width)), fixed((shards, cols * width // shards // LANES, LANES)), fixed((width, LANES)), fixed(residual.shape)],
            scratch_shapes=[
                pltpu.VMEM((2, total, LANES), jnp.bfloat16),
                pltpu.VMEM((2, total, LANES), jnp.bfloat16),
                pltpu.VMEM((HEAD, total), jnp.bfloat16),
                pltpu.VMEM((total, LANES), jnp.float32),
                pltpu.VMEM((total, LANES), jnp.float32),
                pltpu.VMEM((blocks, span, LANES), jnp.float32),
                pltpu.VMEM((LANES, span), jnp.float32),
                pltpu.VMEM((cols, width), jnp.float32),
                pltpu.VMEM(w_out.shape, jnp.float32),
                pltpu.VMEM((2, total, span), jnp.bfloat16),
                pltpu.VMEM((2, total, span), jnp.bfloat16),
            ]
            + Collect.boxes(shards, *residual.shape),
        ),
        out_shape=[
            shape((blocks, span, width), jnp.bfloat16),
            shape((shards, cols * width // shards // LANES, LANES), jnp.bfloat16),
            shape((width, LANES), jnp.bfloat16),
            shape(residual.shape, jnp.bfloat16),
        ],
        compiler_params=remote_params(5, 60),
        cost_estimate=cost(34),
        name="attend_backward",
    )(d_attn, q, kv, mix, lse, start, w_out, w, cut(first), cut(cosine), cut(sine), o_parts, residual)


MESH = pl.DeviceIdType.MESH


def chip_spot():
    me = lax.axis_index("shard")
    return me, me // 2, me % 2


def greet(others):
    barrier = pltpu.get_barrier_semaphore()
    for other in others:
        pl.semaphore_signal(barrier, inc=1, device_id=other, device_id_type=MESH)
    pl.semaphore_wait(barrier, len(others))


def greet_shard(shards):
    me = lax.axis_index("shard")
    greet([{"shard": lax.rem(me + k, shards)} for k in range(1, shards)])


def remote(src, dst, send_sem, recv_sem, target):
    return pltpu.make_async_remote_copy(
        src_ref=src,
        dst_ref=dst,
        send_sem=send_sem,
        recv_sem=recv_sem,
        device_id=target,
        device_id_type=MESH,
    )


def halves(rows):
    first = rows // 32 * 16
    return [(0, first), (first, rows - first)]


class Spread:
    def __init__(self, chips, src, out, sems):
        self.chips, self.src, self.out = chips, src, out
        self.own_sem, self.right_sem, self.left_sem, self.cross_sem, self.recv_sem = sems
        self.me, self.chip, self.core = chip_spot()
        self.cuts = halves(out.shape[1])
        self.has_right, self.has_left = self.chip < chips - 1, self.chip > 0

    @staticmethod
    def sems(shards):
        dma = pltpu.SemaphoreType.DMA
        return [dma((2,)), dma((shards,)), dma((shards,)), dma((shards,)), dma((2 * shards,))]

    def copy(self, way, source, cut, from_src=False, core=None):
        block = 2 * source + (self.core if core is None else core)
        here = pl.ds(*self.cuts[cut])
        sem = dict(right=self.right_sem, left=self.left_sem, cross=self.cross_sem)[way].at[2 * source + cut]
        target = dict(right=self.me + 2, left=self.me - 2, cross=2 * self.chip + 1 - self.core)[way]
        held = self.src.at[here] if from_src else self.out.at[block, here]
        return remote(held, self.out.at[block, here], sem, self.recv_sem.at[2 * block + cut], {"shard": target})

    def own(self, cut):
        here = pl.ds(*self.cuts[cut])
        return pltpu.make_async_copy(self.src.at[here], self.out.at[self.me, here], self.own_sem.at[cut])

    def start(self, cut):
        pl.when(self.has_right)(lambda: self.copy("right", self.chip, cut, True).start())
        pl.when(self.has_left)(lambda: self.copy("left", self.chip, cut, True).start())
        self.copy("cross", self.chip, cut, True).start()
        self.own(cut).start()

    def each(self, action, tick=lambda: None):
        for hop in range(1, self.chips):
            for cut in range(2):
                for side in (-1, 1):
                    source = self.chip + side * hop
                    inside = (source >= 0) if side < 0 else (source < self.chips)
                    pl.when(inside)(functools.partial(action, source, side, cut))
                    tick()

    def carry(self, tick=lambda: None):
        def pass_on(source, side, cut):
            self.copy("cross", source, cut).wait_recv()
            if side < 0:
                pl.when(self.has_right)(lambda: self.copy("right", source, cut).start())
            else:
                pl.when(self.has_left)(lambda: self.copy("left", source, cut).start())
            self.copy("cross", source, cut).start()

        self.each(pass_on, tick)

    def settle(self):
        for source in range(self.chips):
            for cut in range(2):
                self.copy("cross", source, cut, core=1 - self.core).wait_recv()
        for cut in range(2):
            self.own(cut).wait()
            self.copy("cross", self.chip, cut, True).wait_send()
            pl.when(self.has_right)(lambda cut=cut: self.copy("right", self.chip, cut, True).wait_send())
            pl.when(self.has_left)(lambda cut=cut: self.copy("left", self.chip, cut, True).wait_send())

        def sent(source, side, cut):
            if side < 0:
                pl.when(self.has_right)(lambda: self.copy("right", source, cut).wait_send())
            else:
                pl.when(self.has_left)(lambda: self.copy("left", source, cut).wait_send())
            self.copy("cross", source, cut).wait_send()

        self.each(sent)


STRIP = 16


class Collect:
    def __init__(self, chips, parts, boxes):
        self.chips, self.parts = chips, parts
        self.mine, self.cross, self.inbox = boxes[:3]
        self.mine_sem, self.swap_send, self.swap_recv, self.on_send, self.right_recv, self.left_recv = boxes[3:]
        self.me, self.chip, self.core = chip_spot()
        self.cuts = halves(parts.shape[1])

    @staticmethod
    def boxes(shards, rows, width):
        chips = shards // 2
        box = lambda count: pltpu.VMEM((count, rows, width), jnp.bfloat16)
        dma = pltpu.SemaphoreType.DMA
        return [box(chips), box(chips), box(chips + 1), dma((chips,))] + [dma((shards,))] * 5

    def load(self, dest):
        return pltpu.make_async_copy(self.parts.at[2 * dest + self.core], self.mine.at[dest], self.mine_sem.at[dest])

    def swap(self, dest, cut):
        here, sem = pl.ds(*self.cuts[cut]), 2 * dest + cut
        return remote(
            self.parts.at[2 * dest + 1 - self.core, here], self.cross.at[dest, here],
            self.swap_send.at[sem], self.swap_recv.at[sem], {"shard": 2 * self.chip + 1 - self.core},
        )

    def slot(self, dest, side, chip):
        return dest if side > 0 else jnp.where(dest == chip, self.chips, dest)

    def onward(self, dest, side, cut):
        here, at = pl.ds(*self.cuts[cut]), 2 * dest + cut
        slot = self.slot(dest, side, self.chip + side)
        sem, target = (self.right_recv, self.me + 2) if side > 0 else (self.left_recv, self.me - 2)
        return remote(
            self.cross.at[dest, here], self.inbox.at[slot, here], self.on_send.at[at], sem.at[at], {"shard": target}
        )

    def arrived(self, dest, side, cut):
        here, at = pl.ds(*self.cuts[cut]), 2 * dest + cut
        box = self.inbox.at[self.slot(dest, side, self.chip)]
        sem = self.right_recv if side > 0 else self.left_recv
        remote(box.at[here], box.at[here], self.on_send.at[at], sem.at[at], {"shard": 2 * self.chip + 1 - self.core}).wait_recv()
        return box

    def each(self, action, hops=None, tick=lambda: None):
        for hop in range(self.chips - 1, 0, -1) if hops is None else hops:
            for cut in range(2):
                for side in (1, -1):
                    dest = self.chip + side * hop
                    inside = (dest < self.chips) if side > 0 else (dest >= 0)
                    pl.when(inside)(functools.partial(action, dest, side, cut))
                    tick()

    def start(self):
        def begin(dest, side, cut):
            self.swap(dest, cut).start()
            if cut == 0:
                self.load(dest).start()

        self.each(begin)
        for cut in range(2):
            self.swap(self.chip, cut).start()
        self.load(self.chip).start()

    def strips(self, cut, parts, store):
        base, size = self.cuts[cut]

        def body(i, c):
            here = pl.ds(pl.multiple_of(base + i * STRIP, STRIP), STRIP)
            total = parts[0][here].astype(jnp.float32)
            for part in parts[1:]:
                total = total + part[here].astype(jnp.float32)
            store(here, total)
            return c

        lax.fori_loop(0, size // STRIP, body, 0)

    def carry(self, hops=None, tick=lambda: None):
        def pass_on(dest, side, cut):
            if cut == 0:
                self.load(dest).wait()
            self.swap(dest, cut).wait_recv()
            inner = (self.chip > 0) if side > 0 else (self.chip < self.chips - 1)
            near = (self.mine.at[dest], self.cross.at[dest])

            def keep(here, total):
                self.cross[dest, here] = total.astype(jnp.bfloat16)

            pl.when(inner)(lambda: self.strips(cut, near + (self.arrived(dest, side, cut),), keep))
            pl.when(jnp.logical_not(inner))(lambda: self.strips(cut, near, keep))
            self.onward(dest, side, cut).start()

        self.each(pass_on, hops, tick)

    def finish(self, cut, store):
        chip = self.chip
        if cut == 0:
            self.load(chip).wait()
        self.swap(chip, cut).wait_recv()
        near = (self.mine.at[chip], self.cross.at[chip])

        @pl.when((chip > 0) & (chip < self.chips - 1))
        def _():
            both = (self.arrived(chip, 1, cut), self.arrived(chip, -1, cut))
            self.strips(cut, near + both, store)

        pl.when(chip == 0)(lambda: self.strips(cut, near + (self.arrived(chip, -1, cut),), store))
        pl.when(chip == self.chips - 1)(lambda: self.strips(cut, near + (self.arrived(chip, 1, cut),), store))

    def settle(self):
        for cut in range(2):
            self.swap(self.chip, cut).wait_send()
        self.each(lambda dest, side, cut: self.swap(dest, cut).wait_send())
        self.each(lambda dest, side, cut: self.onward(dest, side, cut).wait_send())


class Direct:
    def __init__(self, shards, src, out, send_sem, recv_sem):
        self.shards, self.src, self.out, self.send_sem, self.recv_sem = shards, src, out, send_sem, recv_sem
        self.me = lax.axis_index("shard")

    @staticmethod
    def sems(shards):
        return [pltpu.SemaphoreType.DMA((shards,)), pltpu.SemaphoreType.DMA((shards,))]

    def copy(self, k):
        target = lax.rem(self.me + k, self.shards)
        return remote(
            self.src(target), self.out(self.me), self.send_sem.at[k], self.recv_sem.at[self.me], {"shard": target}
        )

    def own(self):
        return pltpu.make_async_copy(self.src(self.me), self.out(self.me), self.send_sem.at[0])

    def start(self):
        self.own().start()
        for k in range(1, self.shards):
            self.copy(k).start()

    def settle(self):
        self.own().wait()
        for k in range(1, self.shards):
            source = lax.rem(self.me + k, self.shards)
            block = self.out(source)
            remote(block, block, self.send_sem.at[k], self.recv_sem.at[source], {"shard": source}).wait_recv()
        for k in range(1, self.shards):
            self.copy(k).wait_send()


ANY = pl.BlockSpec(memory_space=pl.ANY)
INNER = pl.BlockSpec(memory_space=pltpu.VMEM)


def remote_params(call, megabytes):
    return pltpu.CompilerParams(collective_id=call, has_side_effects=True, vmem_limit_bytes=megabytes << 20)


def cost(micros):
    return pl.CostEstimate(flops=0, bytes_accessed=int(micros * 3.2e6), transcendentals=0)


def open_kernel(shards, x_ref, small_ref, choice_ref, piece_ref, all_x, all_small, all_choice, all_piece, *sems):
    greet_shard(shards)
    spread = Spread(shards // 2, x_ref, all_x, sems[:5])
    for cut in range(2):
        spread.start(cut)
    direct = [
        Direct(shards, lambda target: piece_ref.at[target], lambda source: all_piece.at[source], *sems[5:7]),
        Direct(shards, lambda target: small_ref, lambda source: all_small.at[source], *sems[7:9]),
        Direct(shards, lambda target: choice_ref, lambda source: all_choice.at[source], *sems[9:11]),
    ]
    for one in direct:
        one.start()
    spread.carry()
    for one in direct:
        one.settle()
    spread.settle()


def open_gathers(x, small, choice, pieces, shards):
    wide = lambda a: jax.ShapeDtypeStruct((shards,) + a.shape, a.dtype)
    return pl.pallas_call(
        functools.partial(open_kernel, shards),
        out_shape=[wide(x), wide(small), wide(choice), jax.ShapeDtypeStruct(pieces.shape, pieces.dtype)],
        in_specs=[ANY] * 4,
        out_specs=[ANY] * 4,
        scratch_shapes=Spread.sems(shards) + Direct.sems(shards) * 3,
        compiler_params=remote_params(1, 60),
        cost_estimate=cost(45),
        name="open_gathers",
    )(x, small, choice, pieces)


def expert_ids(shape, per_row):
    row = lax.broadcasted_iota(jnp.int32, shape, 0)
    rows = EXPERTS // per_row
    return per_row * (row % rows) + row // rows


def gate_columns(logits, choice, ids):
    named = jnp.zeros(logits.shape, jnp.float32)
    for k in range(choice.shape[0]):
        named = jnp.where(choice[k : k + 1] == ids, 1.0, named)
    masked = jnp.where(named > 0, logits, NEG)
    weight = jnp.where(named > 0, jnp.exp(masked - jnp.max(masked, axis=0, keepdims=True)), 0.0)
    return weight / jnp.sum(weight, axis=0, keepdims=True)


def middle_kernel(
    shards, parts_ref, x_ref, gain_ref, router_ref, choice_ref, residual_ref, second_ref, gates_ref, all_ref, *scratch
):
    greet_shard(shards)
    chips = shards // 2
    collect = Collect(chips, parts_ref, scratch[:9])
    spread = Spread(chips, second_ref, all_ref, scratch[9:14])
    collect.start()
    collect.carry()
    for cut in range(2):

        def store(here, total):
            residual = x_ref[here].astype(jnp.float32) + total
            residual_ref[here] = residual
            inv = lax.rsqrt(jnp.mean(residual * residual, axis=1, keepdims=True) + EPSILON)
            second_ref[here] = (residual * inv * gain_ref[...]).astype(jnp.bfloat16)

        collect.finish(cut, store)
        spread.start(cut)
    logits = nt_dot(router_ref[...], second_ref[...])
    per_row = x_ref.shape[1] // x_ref.shape[0]
    gates_ref[...] = gate_columns(logits, choice_ref[...], expert_ids(logits.shape, per_row))
    spread.carry()
    collect.settle()
    spread.settle()


def middle(parts, x, gain, router_t, choice_t, shards):
    rows, width = x.shape
    shape = jax.ShapeDtypeStruct
    return pl.pallas_call(
        functools.partial(middle_kernel, shards),
        out_shape=[
            shape((rows, width), jnp.float32),
            shape((rows, width), jnp.bfloat16),
            shape((EXPERTS, rows), jnp.float32),
            shape((shards, rows, width), jnp.bfloat16),
        ],
        in_specs=[ANY] + [INNER] * 4,
        out_specs=[INNER] * 3 + [ANY],
        scratch_shapes=Collect.boxes(shards, rows, width) + Spread.sems(shards),
        compiler_params=remote_params(2, 60),
        cost_estimate=cost(75),
        name="middle",
    )(parts.reshape(shards, rows, width), x, gain, router_t, choice_t)


def turn_kernel(
    shards, reps, parts_ref, gd_ref, residual_ref, cot_ref, gain_ref, gates_ref, second_ref, router_ref,
    dres_ref, dgain_ref, drouter_ref, all_ref, gdsum_ref, dsec_s, datt_s, *scratch
):
    me = lax.axis_index("shard")
    greet([{"shard": lax.rem(me + k, shards)} for k in range(1, shards)] + Exchange.partners(reps))
    chips = shards // 2
    rows, width = residual_ref.shape
    collect = Collect(chips, parts_ref, scratch[:9])
    spread = Spread(chips, datt_s, all_ref, scratch[9:14])
    sums = GridSum(reps, [(gd_ref.at[e], gdsum_ref.at[e]) for e in range(gd_ref.shape[0])], scratch[14:23])
    collect.start()
    sums.begin()
    steps = sums.steps()
    tick = lambda: next(steps, None)
    collect.carry(tick=tick)

    def stash(here, total):
        dsec_s[here] = total

    for cut in range(2):
        collect.finish(cut, stash)
    lines = EXPERTS * rows // width
    d_gates = dsec_s[rows : rows + lines] + dsec_s[rows + lines : rows + 2 * lines]
    d_gates = jnp.concatenate([d_gates[:, k * rows : (k + 1) * rows] for k in range(width // rows)], axis=0)
    gates = gates_ref[...]
    d_logits = gates * (d_gates - jnp.sum(gates * d_gates, axis=0, keepdims=True))
    high = d_logits.astype(jnp.bfloat16)
    low = (d_logits - high.astype(jnp.float32)).astype(jnp.bfloat16)
    drouter_ref[...] = nn_dot(high, second_ref[...]) + nn_dot(low, second_ref[...])
    dgain_ref[...] = jnp.zeros_like(dgain_ref)
    high_t = jnp.transpose(high.astype(jnp.float32)).astype(jnp.bfloat16)
    low_t = jnp.transpose(low.astype(jnp.float32)).astype(jnp.bfloat16)
    for cut in range(2):
        half = rows // 2
        for k in range(2):
            here = slice(cut * half + k * half // 2, cut * half + (k + 1) * half // 2)
            d_second = dsec_s[here] + nn_dot(high_t[here], router_ref[...]) + nn_dot(low_t[here], router_ref[...])
            residual = residual_ref[here]
            inv = lax.rsqrt(jnp.mean(residual * residual, axis=1, keepdims=True) + EPSILON)
            normed = residual * inv
            dgain_ref[...] += jnp.sum(d_second * normed, axis=0, keepdims=True)
            d_norm = d_second * gain_ref[...]
            d_residual = cot_ref[here].astype(jnp.float32) + inv * (
                d_norm - normed * jnp.mean(d_norm * normed, axis=1, keepdims=True)
            )
            dres_ref[here] = d_residual
            datt_s[here] = d_residual.astype(jnp.bfloat16)
        spread.start(cut)
    spread.carry(tick)
    for unused in steps:
        pass
    collect.settle()
    spread.settle()


def turn(parts, grad_down, residual, cot, gain, gates, second, router_t, shards, reps):
    rows, width = residual.shape
    shape = jax.ShapeDtypeStruct
    return pl.pallas_call(
        functools.partial(turn_kernel, shards, reps),
        out_shape=[
            shape((rows, width), jnp.float32),
            shape((1, width), jnp.float32),
            shape((EXPERTS, width), jnp.float32),
            shape((shards, rows, width), jnp.bfloat16),
            shape(grad_down.shape, jnp.bfloat16),
        ],
        in_specs=[ANY] * 2 + [INNER] * 6,
        out_specs=[INNER] * 3 + [ANY] * 2,
        scratch_shapes=[
            pltpu.VMEM((parts.shape[1], width), jnp.float32),
            pltpu.VMEM((rows, width), jnp.bfloat16),
        ]
        + Collect.boxes(shards, parts.shape[1], width)
        + Spread.sems(shards)
        + GridSum.scratch(reps, grad_down.shape[0], grad_down.shape[1], width),
        compiler_params=remote_params(3, 60),
        cost_estimate=cost(75),
        name="turn",
    )(parts, grad_down, residual, cot, gain, gates, second, router_t)


class Exchange:
    def __init__(self, reps, data, boxes, send_sem, recv_sem):
        self.data, self.boxes, self.send_sem, self.recv_sem = data, boxes, send_sem, recv_sem
        self.rep = lax.axis_index("rep")
        self.bits = reps.bit_length() - 1
        half = data.shape[0] // 2
        self.cuts = [(0, half), (half, half)]

    @staticmethod
    def scratch(reps, rows, dtype):
        bits = reps.bit_length() - 1
        dma = pltpu.SemaphoreType.DMA((2 * bits,))
        return [pltpu.VMEM((bits, rows, LANES), dtype), dma, dma]

    @staticmethod
    def partners(reps):
        rep = lax.axis_index("rep")
        bits = [1 << k for k in range(reps.bit_length() - 1)]
        return [{"rep": rep + bit - 2 * bit * ((rep // bit) % 2)} for bit in bits]

    def copy(self, stage, cut):
        here, sem = pl.ds(*self.cuts[cut]), 2 * stage + cut
        bit = 1 << (stage if cut == 0 else self.bits - 1 - stage)
        other = self.rep + bit - 2 * bit * ((self.rep // bit) % 2)
        return remote(
            self.data.at[here], self.boxes.at[stage, here], self.send_sem.at[sem], self.recv_sem.at[sem], {"rep": other}
        )

    def run(self, store):
        for cut in range(2):
            self.copy(0, cut).start()
        for stage in range(self.bits):
            for cut in range(2):
                copy = self.copy(stage, cut)
                copy.wait_recv()
                copy.wait_send()
                base, size = self.cuts[cut]
                strip = 64 if size % 64 == 0 else size

                def body(i, c):
                    here = pl.ds(pl.multiple_of(base + i * strip, 8), strip)
                    total = self.data[here].astype(jnp.float32) + self.boxes[stage, here].astype(jnp.float32)
                    if stage == self.bits - 1:
                        store(here, total)
                    else:
                        self.data[here] = total.astype(self.data.dtype)
                    return c

                lax.fori_loop(0, size // strip, body, 0)
                if stage < self.bits - 1:
                    self.copy(stage + 1, cut).start()


class GridSum:
    def __init__(self, reps, pieces, scratch):
        self.pieces, self.bits = pieces, reps.bit_length() - 1
        self.full, self.inbox, self.result = scratch[:3]
        self.load_sem, self.store_sem, self.down_send, self.down_recv, self.up_send, self.up_recv = scratch[3:]
        self.rep = lax.axis_index("rep")
        self.rows = self.full.shape[1]

    @staticmethod
    def scratch(reps, count, rows, width):
        bits = reps.bit_length() - 1
        dma = pltpu.SemaphoreType.DMA
        return [
            pltpu.VMEM((count, rows, width), jnp.bfloat16),
            pltpu.VMEM((count, rows, width), jnp.bfloat16),
            pltpu.VMEM((count, rows, width), jnp.bfloat16),
            dma((count,)),
            dma((count,)),
        ] + [dma((count, bits))] * 4

    def spot(self, piece, stage):
        base, size = 0, self.rows
        bits = []
        for k in range(stage + 1):
            which = k if piece % 2 == 0 else self.bits - 1 - k
            bits.append((which, (self.rep // (1 << which)) % 2))
        for which, bit in bits[:-1]:
            size //= 2
            base = base + bit * size
        which, bit = bits[-1]
        size //= 2
        kept = pl.multiple_of(base + bit * size, size)
        given = pl.multiple_of(base + (1 - bit) * size, size)
        partner = self.rep + (1 << which) - 2 * (1 << which) * bit
        return kept, given, size, {"rep": partner}

    def box_at(self, stage):
        return sum(self.rows >> (k + 1) for k in range(stage))

    def down(self, piece, stage):
        kept, given, size, partner = self.spot(piece, stage)
        return remote(
            self.full.at[piece, pl.ds(given, size)], self.inbox.at[piece, pl.ds(self.box_at(stage), size)],
            self.down_send.at[piece, stage], self.down_recv.at[piece, stage], partner,
        )

    def up(self, piece, stage, given=False):
        kept, other, size, partner = self.spot(piece, stage)
        here = self.result.at[piece, pl.ds(other if given else kept, size)]
        return remote(here, here, self.up_send.at[piece, stage], self.up_recv.at[piece, stage], partner)

    def load(self, piece):
        return pltpu.make_async_copy(self.pieces[piece][0], self.full.at[piece], self.load_sem.at[piece])

    def store(self, piece):
        return pltpu.make_async_copy(self.result.at[piece], self.pieces[piece][1], self.store_sem.at[piece])

    def add(self, piece, stage):
        kept, given, size, partner = self.spot(piece, stage)
        strip = 32

        def body(i, c):
            here = pl.ds(pl.multiple_of(kept + i * strip, strip), strip)
            there = pl.ds(pl.multiple_of(self.box_at(stage) + i * strip, strip), strip)
            total = self.full[piece, here].astype(jnp.float32) + self.inbox[piece, there].astype(jnp.float32)
            held = self.result if stage == self.bits - 1 else self.full
            held[piece, here] = total.astype(jnp.bfloat16)
            return c

        lax.fori_loop(0, size // strip, body, 0)

    def begin(self):
        for piece in range(len(self.pieces)):
            self.load(piece).start()
        for piece in range(len(self.pieces)):
            self.load(piece).wait()
            self.down(piece, 0).start()

    def steps(self):
        count, bits = len(self.pieces), self.bits
        for stage in range(bits):
            for piece in range(count):
                self.down(piece, stage).wait_recv()
                self.add(piece, stage)
                (self.down(piece, stage + 1) if stage < bits - 1 else self.up(piece, stage)).start()
                yield
        for stage in range(bits - 1, -1, -1):
            for piece in range(count):
                self.up(piece, stage, True).wait_recv()
                (self.up(piece, stage - 1) if stage else self.store(piece)).start()
                yield
        for piece in range(count):
            for stage in range(bits):
                self.down(piece, stage).wait_send()
                self.up(piece, stage).wait_send()
            self.store(piece).wait()


MINI = 48


def close_kernel(
    shards, reps, dparts_ref, x_ref, dres_ref, gain_ref, head_ref, outg_ref, drouter_ref,
    dgain_ref, dtok_ref, share_ref, small_ref, bulk_s, mini_s, sum_s, minis_s, *scratch
):
    me = lax.axis_index("shard")
    greet([{"shard": lax.rem(me + k, shards)} for k in range(1, shards)] + Exchange.partners(reps))
    chips = shards // 2
    tok = Collect(chips, dparts_ref, scratch[:9])
    piece = head_ref.shape[1]
    bulk_at = lambda source: bulk_s.at[pl.ds(pl.multiple_of(source * piece, piece), piece)]
    heads = Direct(shards, lambda target: head_ref.at[target], bulk_at, *scratch[9:11])
    mini = Direct(shards, lambda target: mini_s.at[target], lambda source: minis_s.at[source], *scratch[11:13])
    bulk_sum = Exchange(reps, bulk_s, *scratch[13:16])
    mini_sum = Exchange(reps, sum_s, *scratch[16:19])
    tok.start()
    heads.start()
    bulk_s[shards * piece :] = outg_ref[...]
    cols = gain_ref.shape[1] // shards
    mini_s[...] = jnp.zeros_like(mini_s)
    for k in range(shards):
        here = slice(k * cols, (k + 1) * cols)
        mini_s[k, :EXPERTS, :cols] = drouter_ref[:, here]
        mini_s[k, EXPERTS : EXPERTS + 1, :cols] = dgain_ref[:, here]
    tok.carry()

    def finish_tok(here, d_first):
        x = x_ref[here].astype(jnp.float32)
        inv = lax.rsqrt(jnp.mean(x * x, axis=1, keepdims=True) + EPSILON)
        normed = x * inv
        term = jnp.sum(d_first * normed, axis=0, keepdims=True)
        for k in range(shards):
            mini_s[k, EXPERTS + 1 : EXPERTS + 2, :cols] += term[:, k * cols : (k + 1) * cols]
        d_norm = d_first * gain_ref[...]
        dtok_ref[here] = dres_ref[here] + inv * (d_norm - normed * jnp.mean(d_norm * normed, axis=1, keepdims=True))

    for cut in range(2):
        tok.finish(cut, finish_tok)
    mini.start()
    heads.settle()

    def keep_bulk(here, total):
        share_ref[here] = total

    bulk_sum.run(keep_bulk)
    mini.settle()
    total = minis_s[0]
    for k in range(1, shards):
        total = total + minis_s[k]
    sum_s[...] = total

    def keep_mini(here, total):
        small_ref[here] = total

    mini_sum.run(keep_mini)
    tok.settle()


def close(d_parts, x, d_residual, gain, head_parts, out_grad, d_router, d_gain, shards, reps):
    rows, width = x.shape
    shape = jax.ShapeDtypeStruct
    piece = head_parts.shape[1]
    bulk = shards * piece + out_grad.shape[0]
    f32, bf16 = jnp.float32, jnp.bfloat16
    deep = lambda a: a.reshape(shards, rows, width)
    return pl.pallas_call(
        functools.partial(close_kernel, shards, reps),
        out_shape=[
            shape((rows, width), f32),
            shape((bulk, LANES), f32),
            shape((MINI, LANES), f32),
        ],
        in_specs=[ANY] + [INNER] * 7,
        out_specs=[INNER] * 3,
        scratch_shapes=[
            pltpu.VMEM((bulk, LANES), bf16),
            pltpu.VMEM((shards, MINI, LANES), f32),
            pltpu.VMEM((MINI, LANES), f32),
            pltpu.VMEM((shards, MINI, LANES), f32),
        ]
        + Collect.boxes(shards, rows, width)
        + Direct.sems(shards) * 2
        + Exchange.scratch(reps, bulk, bf16)
        + Exchange.scratch(reps, MINI, f32),
        compiler_params=remote_params(4, 60),
        cost_estimate=cost(70),
        name="close",
    )(deep(d_parts), x, d_residual, gain, head_parts, out_grad, d_router, d_gain)


def tn_dot(a, b):
    return lax.dot_general(a, b, (((0,), (0,)), ((), ())), preferred_element_type=jnp.float32)


def slot_picks(choice, first_expert, local):
    rows = choice.shape[1]
    named = []
    for e in range(8):
        hit = jnp.zeros((1, rows), jnp.float32)
        if e < local:
            hit = jnp.max(jnp.where(choice == first_expert + e, 1.0, 0.0), axis=0, keepdims=True)
        named.append(hit)
    named = jnp.concatenate(named, axis=0)
    earlier = lax.broadcasted_iota(jnp.int32, (rows, rows), 0) < lax.broadcasted_iota(jnp.int32, (rows, rows), 1)
    rank = nn_dot(named.astype(jnp.bfloat16), jnp.where(earlier, 1.0, 0.0).astype(jnp.bfloat16))
    rank = jnp.where(named > 0, rank, -1.0)
    slot = lax.broadcasted_iota(jnp.int32, (CAP, rows), 0).astype(jnp.float32)
    return [jnp.where(rank[e : e + 1] == slot, 1.0, 0.0) for e in range(local)]


def pick_kernel(first_ref, x_ref, g_ref, choice_ref, router_ref, xs_ref, gs_ref, gate_ref):
    local = xs_ref.shape[0]
    rows = x_ref.shape[1]
    x, choice, first_expert = x_ref[0], choice_ref[0], first_ref[0]
    logits = nt_dot(router_ref[...], x)
    ids = expert_ids(logits.shape, x.shape[1] // x.shape[0])
    gates = gate_columns(logits, choice, ids)
    picks = slot_picks(choice, first_expert, local)
    for e in range(local):
        own = jnp.sum(jnp.where(ids == first_expert + e, gates, 0.0), axis=0, keepdims=True)
        gate_ref[e, 0] = jnp.sum(picks[e] * own, axis=1, keepdims=True)
    pick = jnp.concatenate(picks, axis=0).astype(jnp.bfloat16)
    xs = nn_dot(pick, x).astype(jnp.bfloat16)
    gs = nn_dot(pick, g_ref[0]).astype(jnp.bfloat16)
    for e in range(local):
        xs_ref[e, 0] = xs[e * CAP : (e + 1) * CAP]
        gs_ref[e, 0] = gs[e * CAP : (e + 1) * CAP]


def expert_kernel(xs_ref, gs_ref, gate_ref, wgu_ref, wd_ref, y_ref, dy_ref, dgate_ref, ggu_ref, gd_ref, hid_s, dg_s, dgu_s):
    slots = xs_ref.shape[1]
    chunk = 256

    def part(i, c):
        here = pl.ds(pl.multiple_of(i * chunk, chunk), chunk)
        gate = gate_ref[0, here]
        gate_up = nn_dot(xs_ref[0, here], wgu_ref[0])
        gate_part, up_part = gate_up[:, :FF], gate_up[:, FF:]
        sig = 1.0 / (1.0 + jnp.exp(-gate_part))
        silu = gate_part * sig
        hidden = (silu * up_part).astype(jnp.bfloat16)
        hid_s[here] = hidden
        out = nn_dot(hidden, wd_ref[0])
        g = gs_ref[0, here].astype(jnp.float32)
        dgate_ref[0, here] = jnp.sum(out * g, axis=1, keepdims=True)
        y_ref[0, here] = (out * gate).astype(jnp.bfloat16)
        d_out = (g * gate).astype(jnp.bfloat16)
        dg_s[here] = d_out
        d_hidden = nt_dot(d_out, wd_ref[0])
        d_up = (d_hidden * silu).astype(jnp.bfloat16)
        d_gate = (d_hidden * up_part * (sig * (1.0 + gate_part * (1.0 - sig)))).astype(jnp.bfloat16)
        dgu = jnp.concatenate([d_gate, d_up], axis=1)
        dgu_s[here] = dgu
        dy_ref[0, here] = nt_dot(dgu, wgu_ref[0]).astype(jnp.bfloat16)
        return c

    lax.fori_loop(0, slots // chunk, part, 0)
    cols = 256
    for k in range(hid_s.shape[1] // cols):
        here = slice(k * cols, (k + 1) * cols)
        gd_ref[0, here, :] = tn_dot(hid_s[:, here], dg_s[...]).astype(jnp.bfloat16)
    for k in range(xs_ref.shape[2] // cols):
        here = slice(k * cols, (k + 1) * cols)
        ggu_ref[0, here, :] = tn_dot(xs_ref[0, :, here], dgu_s[...]).astype(jnp.bfloat16)


def combine_kernel(first_ref, choice_ref, y_ref, dy_ref, dgate_ref, out_ref, dout_ref):
    local = y_ref.shape[0]
    rows, width = out_ref.shape[1:]
    first_expert = first_ref[0]
    picks = slot_picks(choice_ref[0], first_expert, local)
    per_row = width // rows
    lines = EXPERTS // per_row
    line = lax.broadcasted_iota(jnp.int32, (lines, rows), 0)
    spots = [jnp.zeros((lines, rows), jnp.float32)] * per_row
    for e in range(local):
        d_gate = jnp.sum(picks[e] * dgate_ref[e, 0], axis=0, keepdims=True)
        for k in range(per_row):
            spots[k] = jnp.where(line * per_row + k == first_expert + e, d_gate, spots[k])
    d_gates = jnp.concatenate(spots, axis=1)
    high = d_gates.astype(jnp.bfloat16)
    low = (d_gates - high.astype(jnp.float32)).astype(jnp.bfloat16)
    dout_ref[0, rows:] = jnp.concatenate([high.astype(jnp.float32), low.astype(jnp.float32)], axis=0).astype(jnp.bfloat16)
    pick = jnp.concatenate(picks, axis=0).astype(jnp.bfloat16)
    out_ref[0] = tn_dot(pick, y_ref[:, 0].reshape(local * CAP, -1)).astype(jnp.bfloat16)
    dout_ref[0, :rows] = tn_dot(pick, dy_ref[:, 0].reshape(local * CAP, -1)).astype(jnp.bfloat16)


def run_experts(group_in, group_cot, group_choice, router_t, w_gate_up, w_down, first_expert):
    shards, rows, width = group_in.shape
    local = w_down.shape[0]
    slots = shards * CAP
    shape = jax.ShapeDtypeStruct
    params = lambda mb: pltpu.CompilerParams(dimension_semantics=("arbitrary",), vmem_limit_bytes=mb << 20)
    source = pl.BlockSpec((1, rows, width), lambda n, first: (n, 0, 0))
    named = pl.BlockSpec((1, TOPK, rows), lambda n, first: (n, 0, 0))
    placed = pl.BlockSpec((local, 1, CAP, width), lambda n, first: (0, n, 0, 0))
    thin = pl.BlockSpec((local, 1, CAP, 1), lambda n, first: (0, n, 0, 0))
    bf16, f32 = jnp.bfloat16, jnp.float32
    xs, gs, gates = pl.pallas_call(
        pick_kernel,
        grid_spec=pltpu.PrefetchScalarGridSpec(
            num_scalar_prefetch=1,
            grid=(shards,),
            in_specs=[source, source, named, pl.BlockSpec(router_t.shape, lambda n, first: (0, 0))],
            out_specs=[placed, placed, thin],
        ),
        out_shape=[
            shape((local, shards, CAP, width), bf16),
            shape((local, shards, CAP, width), bf16),
            shape((local, shards, CAP, 1), f32),
        ],
        compiler_params=params(60),
        cost_estimate=cost(8),
        name="pick_rows",
    )(first_expert, group_in, group_cot, group_choice, router_t)
    flat = lambda a: a.reshape(local, slots, a.shape[3])
    each = lambda r, c: pl.BlockSpec((1, r, c), lambda e: (e, 0, 0))
    y, dy, dgate, ggu, gd = pl.pallas_call(
        expert_kernel,
        grid=(local,),
        in_specs=[each(slots, width), each(slots, width), each(slots, 1), each(width, 2 * FF), each(FF, width)],
        out_specs=[each(slots, width), each(slots, width), each(slots, 1), each(width, 2 * FF), each(FF, width)],
        out_shape=[
            shape((local, slots, width), bf16),
            shape((local, slots, width), bf16),
            shape((local, slots, 1), f32),
            shape(w_gate_up.shape, bf16),
            shape(w_down.shape, bf16),
        ],
        scratch_shapes=[
            pltpu.VMEM((slots, FF), bf16),
            pltpu.VMEM((slots, width), bf16),
            pltpu.VMEM((slots, 2 * FF), bf16),
        ],
        compiler_params=params(60),
        cost_estimate=cost(42),
        name="experts",
    )(flat(xs), flat(gs), flat(gates), w_gate_up, w_down)
    deep = lambda a: a.reshape(local, shards, CAP, a.shape[2])
    extra = 2 * EXPERTS * rows // width
    out, d_out = pl.pallas_call(
        combine_kernel,
        grid_spec=pltpu.PrefetchScalarGridSpec(
            num_scalar_prefetch=1,
            grid=(shards,),
            in_specs=[named, placed, placed, thin],
            out_specs=[source, pl.BlockSpec((1, rows + extra, width), lambda n, first: (n, 0, 0))],
        ),
        out_shape=[
            shape((shards, rows, width), bf16),
            shape((shards, rows + extra, width), bf16),
        ],
        compiler_params=params(60),
        cost_estimate=cost(9),
        name="combine_rows",
    )(first_expert, group_choice, deep(y), deep(dy), deep(dgate))
    return out, d_out, ggu, gd


def layout(lengths, tok_index, prompt_len):
    order = jnp.arange(lengths.shape[0])
    starts = prompt_len + jnp.sum(jnp.where(order[None, :] < order[:, None], lengths[None, :], 0), axis=1)
    passed = tok_index[:, None] >= starts[None, :]
    seg_start = jnp.max(jnp.where(passed, starts[None, :], 0), axis=1)
    position = jnp.where(seg_start > 0, tok_index - seg_start + prompt_len, tok_index)
    return (seg_start, position)


def head_pieces(w_qkv, shards):
    rows = w_qkv.shape[0]
    query_width, key_width = HEADS * HEAD, KV_HEADS * HEAD
    part = w_qkv[:, :query_width].reshape(rows, shards, query_width // shards)
    part = jnp.pad(part, ((0, 0), (0, 0), (0, LANES - part.shape[2])))
    share = shards // KV_HEADS
    keys = jnp.repeat(
        w_qkv[:, query_width : query_width + key_width].reshape(rows, KV_HEADS, HEAD), share, axis=1
    )
    vals = jnp.repeat(w_qkv[:, query_width + key_width :].reshape(rows, KV_HEADS, HEAD), share, axis=1)
    return jnp.concatenate([part, keys, vals], axis=2).transpose(1, 0, 2)


def joined_heads(pieces, shards):
    rows = pieces.shape[2]
    query_part = HEADS * HEAD // shards
    share = shards // KV_HEADS
    query = pieces[:, :query_part].reshape(HEADS * HEAD, rows)
    key = jnp.sum(pieces[:, LANES : LANES + HEAD].reshape(KV_HEADS, share, HEAD, rows), axis=1)
    val = jnp.sum(pieces[:, LANES + HEAD :].reshape(KV_HEADS, share, HEAD, rows), axis=1)
    joined = jnp.concatenate(
        [query, key.reshape(KV_HEADS * HEAD, rows), val.reshape(KV_HEADS * HEAD, rows)], axis=0
    )
    return joined.T


def on_device(
    tokens, choices, cont_lengths, norm_attn, w_qkv, w_out, norm_ffn, w_router, w_gate_up, w_down, cotangent
):
    row_count, model_width = tokens.shape
    shards, reps = lax.axis_size("shard"), lax.axis_size("rep")
    group_len = row_count * shards
    prompt_len = group_len // 2
    own_rows = norm_attn.shape[0]
    per_row = model_width // row_count
    router_part = w_router.T.reshape(EXPERTS // per_row, per_row, own_rows).transpose(1, 0, 2)
    small = jnp.concatenate(
        [router_part.reshape(EXPERTS, own_rows), norm_attn[None], norm_ffn[None], jnp.zeros((6, own_rows), jnp.bfloat16)],
        axis=0,
    )
    choice_t = choices.T
    group_tokens, group_small, group_choice, w_heads = open_gathers(
        tokens, small, choice_t, head_pieces(w_qkv, shards), shards
    )
    held_cot, group_tokens = lax.optimization_barrier((cotangent, group_tokens))
    group_cot = lax.all_gather(held_cot, "shard", axis=0, tiled=True)
    group_small = group_small.transpose(1, 0, 2).reshape(small.shape[0], model_width)
    router_t = group_small[:EXPERTS]
    gain_attn = group_small[EXPERTS : EXPERTS + 1].astype(jnp.float32)
    gain_ffn = group_small[EXPERTS + 1 : EXPERTS + 2].astype(jnp.float32)
    w_heads = w_heads.reshape(model_width, 2 * LANES)
    own_out = jnp.pad(w_out, ((0, LANES - w_out.shape[0]), (0, 0)))
    group_index = jnp.arange(group_len, dtype=jnp.int32)
    seg_start, position = layout(cont_lengths[0], group_index, prompt_len)
    lane = jnp.arange(LANES, dtype=jnp.int32)
    half = HEAD // 2
    freq_table = 10000.0 ** (-(lane % half).astype(jnp.float32) / half)
    angle = position.astype(jnp.float32)[:, None] * freq_table[None, :]
    cosine = jnp.cos(angle)
    sine = jnp.sin(angle) * jnp.where(lane % HEAD < half, -1.0, 1.0)[None, :]
    start_row = seg_start[None, :]
    cosine, sine, start_row = lax.optimization_barrier((cosine, sine, start_row))
    out_parts, group_first, queries, key_values, mixed_t, log_total = attend_forward(
        group_tokens.reshape(group_len, model_width), gain_attn, w_heads, cosine, sine, own_out, start_row
    )
    residual, second_in, gates, group_in = middle(out_parts, tokens, gain_ffn, router_t, choice_t, shards)
    out_terms, d_terms, grad_gate_up, grad_down = run_experts(
        group_in, group_cot.reshape(group_in.shape), group_choice, router_t, w_gate_up, w_down,
        lax.axis_index("shard")[None] * w_down.shape[0],
    )
    grad_gate_up = lax.psum(grad_gate_up, "rep")
    d_residual, d_gain, d_router, group_d_attn, grad_down = turn(
        d_terms, grad_down, residual, cotangent, gain_ffn, gates, second_in, router_t, shards, reps
    )
    d_parts, head_parts, out_grad, output = attend_backward(
        group_d_attn.reshape(group_len, model_width), queries, key_values, mixed_t, log_total, start_row,
        own_out, w_heads, group_first, cosine, sine, out_terms, residual, shards,
    )
    d_tokens, share, small_sum = close(
        d_parts, tokens, d_residual, gain_attn, head_parts, out_grad, d_router, d_gain, shards, reps
    )
    lines = head_parts.shape[1]
    head_grads = share[: shards * lines].reshape(shards, lines, LANES // own_rows, own_rows)
    head_grads = head_grads.transpose(0, 2, 1, 3).reshape(shards, 2 * LANES, own_rows)
    out_share = share[shards * lines :].reshape(model_width // LANES, LANES, LANES).transpose(1, 0, 2)
    router_share = small_sum[:EXPERTS, :own_rows].reshape(per_row, EXPERTS // per_row, own_rows).transpose(2, 1, 0)
    return (
        output,
        d_tokens,
        small_sum[EXPERTS + 1, :own_rows],
        joined_heads(head_grads, shards),
        out_share.reshape(LANES, model_width)[: w_out.shape[0]],
        small_sum[EXPERTS, :own_rows],
        router_share.reshape(own_rows, EXPERTS),
        grad_gate_up.astype(jnp.float32),
        grad_down.astype(jnp.float32),
    )


def solution(mesh):
    return jax.shard_map(
        on_device,
        mesh=mesh,
        in_specs=(
            P(("rep", "shard"), None),
            P(("rep", "shard"), None),
            P("rep", None),
            P("shard"),
            P("shard", None),
            P("shard", None),
            P("shard"),
            P("shard", None),
            P("shard", None, None),
            P("shard", None, None),
            P(("rep", "shard"), None),
        ),
        out_specs=(
            P(("rep", "shard"), None),
            P(("rep", "shard"), None),
            P("shard"),
            P("shard", None),
            P("shard", None),
            P("shard"),
            P("shard", None),
            P("shard", None, None),
            P("shard", None, None),
        ),
        check_vma=False,
    )
```

```python
import functools

import jax
import jax.numpy as jnp
from jax import lax
from jax.experimental import pallas as pl
from jax.experimental.pallas import tpu as pltpu
from jax.sharding import PartitionSpec as P

HEADS = 16
KV_HEADS = 8
HEAD = 64
EXPERTS = 32
FF = 512
TOPK = 8
CAP = 96
EPSILON = 1e-06


NEG = -1e30
KEYS = 512
LANES = 128


def swap_halves(x):
    lane = lax.broadcasted_iota(jnp.int32, x.shape, 1)
    return jnp.where(lane % HEAD < HEAD // 2, pltpu.roll(x, LANES - HEAD // 2, 1), pltpu.roll(x, HEAD // 2, 1))


def nt_dot(a, b):
    return lax.dot_general(a, b, (((1,), (1,)), ((), ())), preferred_element_type=jnp.float32)


def nn_dot(a, b):
    return jnp.dot(a, b, preferred_element_type=jnp.float32)


def split_kv(kv, low_lane):
    turned = pltpu.roll(kv, HEAD, 1)
    keys = (jnp.where(low_lane, kv, 0.0), jnp.where(low_lane, 0.0, turned))
    vals = (jnp.where(low_lane, turned, 0.0), jnp.where(low_lane, 0.0, kv))
    return keys, vals


def allowed_mask(lo, hi, query_base, start_row):
    key = lo + lax.broadcasted_iota(jnp.int32, (hi - lo, start_row.shape[1]), 0)
    query = query_base + lax.broadcasted_iota(jnp.int32, (hi - lo, start_row.shape[1]), 1)
    return (key <= query) & (key >= start_row)


def causal_chunks(block, prompt_blocks, span):
    free = min(block, prompt_blocks) * span
    end = (block + 1) * span
    cuts = [(k, min(k + KEYS, free), False) for k in range(0, free, KEYS)]
    return cuts + [(k, min(k + KEYS, end), True) for k in range(free, end, KEYS)]


def attend_forward_kernel(
    x_ref, gain_ref, w_ref, cos_ref, sin_ref, wout_ref, start_ref,
    part_ref, first_ref, q_ref, kv_ref, mix_ref, lse_ref,
    keys_s, vals_s, qt_s, s_s, p_s, acc_s,
):
    block = pl.program_id(0)
    span = q_ref.shape[0]
    blocks = keys_s.shape[1] // span
    x = x_ref[...].astype(jnp.float32)
    inv = lax.rsqrt(jnp.mean(x * x, axis=1, keepdims=True) + EPSILON)
    first = (x * inv * gain_ref[...]).astype(jnp.bfloat16)
    first_ref[...] = first
    qkv = nn_dot(first, w_ref[...])
    lane = lax.broadcasted_iota(jnp.int32, (span, LANES), 1)
    low_lane = lane < HEAD
    cosine, sine = cos_ref[...], sin_ref[...]
    q = qkv[:, :LANES]
    q = q * cosine + swap_halves(q) * sine
    kv = qkv[:, LANES:]
    kv = jnp.where(low_lane, kv * cosine + swap_halves(kv) * sine, kv)
    q_ref[...] = q.astype(jnp.bfloat16)
    kv_ref[...] = kv.astype(jnp.bfloat16)
    keys, unused = split_kv(kv, low_lane)
    here = pl.ds(pl.multiple_of(block * span, span), span)
    for h in range(2):
        keys_s[h, here] = keys[h].astype(jnp.bfloat16)
    vals_s[:, here] = jnp.transpose(kv)[HEAD:].astype(jnp.bfloat16)
    qt_s[...] = (jnp.transpose(q.astype(jnp.bfloat16).astype(jnp.float32)) * HEAD**-0.5).astype(jnp.bfloat16)

    def attend(i):
        chunks = causal_chunks(i, blocks // 2, span)
        end = (i + 1) * span
        q_t = qt_s[...]
        start_row = start_ref[...]
        for h in range(2):
            top = jnp.full((1, span), NEG, jnp.float32)
            for lo, hi, masked in chunks:
                s = nn_dot(keys_s[h, lo:hi], q_t)
                if masked:
                    s = jnp.where(allowed_mask(lo, hi, i * span, start_row), s, NEG)
                s_s[h, lo:hi] = s
                top = jnp.maximum(top, jnp.max(s, axis=0, keepdims=True))
            total = jnp.zeros((1, span), jnp.float32)
            for lo, hi, masked in chunks:
                p = jnp.exp(s_s[h, lo:hi] - top)
                total = total + jnp.sum(p, axis=0, keepdims=True)
                p_s[h, lo:hi] = p.astype(jnp.bfloat16)
            acc_s[h * HEAD : (h + 1) * HEAD] = nn_dot(vals_s[:, :end], p_s[h, :end]) / total
            lse_ref[h : h + 1, :] = top + jnp.log(total)

    for i in range(blocks):
        pl.when(block == i)(functools.partial(attend, i))
    mix_t = acc_s[...]
    mix_ref[...] = mix_t.astype(jnp.bfloat16)
    part_ref[...] = nn_dot(jnp.transpose(mix_t).astype(jnp.bfloat16), wout_ref[...]).astype(jnp.bfloat16)


def attend_backward_kernel(
    shards, reps, experts, da_ref, q_ref, kv_ref, mix_ref, lse_ref, start_ref, wout_ref, w_ref, first_ref, cos_ref,
    sin_ref, oparts_ref, residual_ref, gu_in, head_ref, dfirst_ref, gw_ref, gout_ref, out_ref, gu_ref,
    copy_sem,
    keys_s, vals_s, keyt_s, dk_s, dv_s, dq_s, dqt_s, gw_s, gout_s, p_s, ds_s, *scratch
):
    block = pl.program_id(0)
    span = q_ref.shape[0]
    blocks = keys_s.shape[1] // span
    fwd = Collect(shards // 2, oparts_ref, scratch[:9])
    sums = GridSum(reps, gate_up_pieces(gu_ref, experts), scratch[9:18])
    tick, drain = pacer(sums.steps())
    half = gu_ref.shape[1] // 2
    moves = [
        pltpu.make_async_copy(head_ref.at[k], gu_ref.at[0, pl.ds(k * half, half)], copy_sem.at[k]) for k in range(2)
    ]

    @pl.when(block == 0)
    def _():
        me = lax.axis_index("shard")
        greet([{"shard": lax.rem(me + k, shards)} for k in range(1, shards)] + Exchange.partners(reps))
        fwd.start()
        sums.begin()
        for move in moves:
            move.start()

    lane = lax.broadcasted_iota(jnp.int32, (span, LANES), 1)
    low_lane = lane < HEAD

    @pl.when(block == 0)
    def _():
        def prepare(j, c):
            here = pl.ds(pl.multiple_of(j * span, span), span)
            kv = kv_ref[here].astype(jnp.float32)
            keys, vals = split_kv(kv, low_lane)
            for h in range(2):
                keys_s[h, here] = keys[h].astype(jnp.bfloat16)
                vals_s[h, here] = vals[h].astype(jnp.bfloat16)
            keyt_s[:, here] = jnp.transpose(kv)[:HEAD].astype(jnp.bfloat16)
            dk_s[here] = jnp.zeros((span, LANES), jnp.float32)
            dv_s[here] = jnp.zeros((span, LANES), jnp.float32)
            return c

        lax.fori_loop(0, blocks, prepare, 0)
        gout_s[...] = jnp.zeros_like(gout_s)
        gw_s[...] = jnp.zeros_like(gw_s)

    da = da_ref[...]
    dm_f = nt_dot(da, wout_ref[...])
    dm = dm_f.astype(jnp.bfloat16)
    dm_tf = jnp.transpose(dm.astype(jnp.float32))
    dm_t = dm_tf.astype(jnp.bfloat16)
    gout_s[...] += nn_dot(mix_ref[...], da)
    prod = mix_ref[...].astype(jnp.float32) * dm_tf
    delta = [jnp.sum(prod[h * HEAD : (h + 1) * HEAD], axis=0, keepdims=True) for h in range(2)]
    qs_f = q_ref[...].astype(jnp.float32) * HEAD**-0.5
    qs = qs_f.astype(jnp.bfloat16)
    q_t = jnp.transpose(qs_f).astype(jnp.bfloat16)

    def attend(i):
        chunks = causal_chunks(i, blocks // 2, span)
        end = (i + 1) * span
        start_row = start_ref[...]
        for h in range(2):
            for lo, hi, masked in chunks:
                s = nn_dot(keys_s[h, lo:hi], q_t)
                if masked:
                    s = jnp.where(allowed_mask(lo, hi, i * span, start_row), s, NEG)
                p = jnp.exp(s - lse_ref[h : h + 1, :])
                dp = nn_dot(vals_s[h, lo:hi], dm_t)
                p_s[h, lo:hi] = p.astype(jnp.bfloat16)
                ds_s[h, lo:hi] = (p * (dp - delta[h])).astype(jnp.bfloat16)
            dqt_s[h * HEAD : (h + 1) * HEAD] = nn_dot(keyt_s[:, :end], ds_s[h, :end])
        for lo, hi, masked in chunks:
            low_key = lax.broadcasted_iota(jnp.int32, (hi - lo, LANES), 1) < HEAD
            dv_s[lo:hi] += jnp.where(low_key, nn_dot(p_s[0, lo:hi], dm), nn_dot(p_s[1, lo:hi], dm))
            dk_s[lo:hi] += jnp.where(low_key, nn_dot(ds_s[0, lo:hi], qs), nn_dot(ds_s[1, lo:hi], qs))

    for i in range(blocks):
        pl.when(block == i)(functools.partial(attend, i))
    dq_s[block] = jnp.transpose(dqt_s[...]) * HEAD**-0.5
    hops = list(range(shards // 2 - 1, 0, -1))
    turns = {}
    for k, hop in enumerate(hops):
        turns.setdefault(0 if k == 0 else blocks - len(hops) + k, []).append(hop)
    for turn_block, some in turns.items():
        pl.when(block == turn_block)(functools.partial(fwd.carry, some))
    for k in range(1, blocks):

        @pl.when(block == k)
        def _():
            tick(2)


    @pl.when(block == blocks - 1)
    def _():
        def finish(j, c):
            here = pl.ds(pl.multiple_of(j * span, span), span)
            dk = dk_s[here]
            dk = dk + pltpu.roll(dk, HEAD, 1)
            dv = dv_s[here]
            dv = dv + pltpu.roll(dv, HEAD, 1)
            cosine, sine = cos_ref[j], sin_ref[j]
            dkv = jnp.where(low_lane, dk * cosine - swap_halves(dk) * sine, dv).astype(jnp.bfloat16)
            dq = dq_s[j]
            dq = (dq * cosine - swap_halves(dq) * sine).astype(jnp.bfloat16)
            d_qkv = jnp.concatenate([dq, dkv], axis=1)
            d_qkv_t = jnp.transpose(d_qkv.astype(jnp.float32)).astype(jnp.bfloat16)
            gw_s[...] += nn_dot(d_qkv_t, first_ref[j])
            dfirst_ref[j] = nt_dot(d_qkv, w_ref[...]).astype(jnp.bfloat16)
            return c

        lax.fori_loop(0, blocks, finish, 0)
        shards, lines = gw_ref.shape[:2]
        cols = gw_s.shape[1] // shards
        for k in range(shards):
            for p in range(LANES // cols):
                gw_ref[k, :, p * cols : (p + 1) * cols] = gw_s[
                    p * lines : (p + 1) * lines, k * cols : (k + 1) * cols
                ].astype(jnp.bfloat16)
        for k in range(gout_s.shape[1] // LANES):
            gout_ref[k * LANES : (k + 1) * LANES] = gout_s[:, k * LANES : (k + 1) * LANES].astype(jnp.bfloat16)

        def finish_out(here, total):
            out_ref[here] = (residual_ref[here] + total).astype(jnp.bfloat16)

        for cut in range(2):
            fwd.finish(cut, finish_out)
        drain()
        for move in moves:
            move.wait()
        fwd.settle()


def attend_forward(x, gain, w, cosine, sine, w_out, start):
    total, width = x.shape
    span = 512 if total <= 2048 else 256
    blocks = total // span
    row = lambda cols: pl.BlockSpec((span, cols), lambda i: (i, 0))
    col = lambda rows: pl.BlockSpec((rows, span), lambda i: (0, i))
    fixed = lambda shape: pl.BlockSpec(shape, lambda i: tuple(0 for s in shape), pipeline_mode=pl.Buffered(1))
    shape = jax.ShapeDtypeStruct
    return pl.pallas_call(
        attend_forward_kernel,
        grid_spec=pltpu.PrefetchScalarGridSpec(
            num_scalar_prefetch=0,
            grid=(blocks,),
            in_specs=[row(width), fixed((1, width)), fixed(w.shape), row(LANES), row(LANES), fixed(w_out.shape), col(1)],
            out_specs=[row(width), row(width), row(LANES), row(LANES), col(LANES), col(2)],
            scratch_shapes=[
                pltpu.VMEM((2, total, LANES), jnp.bfloat16),
                pltpu.VMEM((HEAD, total), jnp.bfloat16),
                pltpu.VMEM((LANES, span), jnp.bfloat16),
                pltpu.VMEM((2, total, span), jnp.float32),
                pltpu.VMEM((2, total, span), jnp.bfloat16),
                pltpu.VMEM((LANES, span), jnp.float32),
            ],
        ),
        out_shape=[
            shape((total, width), jnp.bfloat16),
            shape((total, width), jnp.bfloat16),
            shape((total, LANES), jnp.bfloat16),
            shape((total, LANES), jnp.bfloat16),
            shape((LANES, total), jnp.bfloat16),
            shape((2, total), jnp.float32),
        ],
        compiler_params=pltpu.CompilerParams(dimension_semantics=("arbitrary",), vmem_limit_bytes=60 << 20),
        cost_estimate=cost(17),
        name="attend_forward",
    )(x, gain, w, cosine, sine, w_out, start)


def attend_backward(
    d_attn, q, kv, mix, lse, start, w_out, w, first, cosine, sine, o_parts, residual, grad_gate_up, experts,
    head_sum, shards, reps,
):
    total, width = d_attn.shape
    span = 512 if total <= 2048 else 256
    blocks = total // span
    cols = w.shape[1]
    row = lambda cols: pl.BlockSpec((span, cols), lambda i: (i, 0))
    col = lambda rows: pl.BlockSpec((rows, span), lambda i: (0, i))
    fixed = lambda shape: pl.BlockSpec(shape, lambda i: tuple(0 for s in shape), pipeline_mode=pl.Buffered(1))
    shape = jax.ShapeDtypeStruct
    cut = lambda a: a.reshape(blocks, span, a.shape[1])
    return pl.pallas_call(
        functools.partial(attend_backward_kernel, shards, reps, experts),
        grid_spec=pltpu.PrefetchScalarGridSpec(
            num_scalar_prefetch=0,
            grid=(blocks,),
            in_specs=[
                row(width), row(LANES), fixed((total, LANES)), col(LANES), col(2), col(1),
                fixed(w_out.shape), fixed(w.shape), fixed((blocks, span, width)),
                fixed((blocks, span, LANES)), fixed((blocks, span, LANES)), ANY, fixed(residual.shape), ANY, ANY,
            ],
            out_specs=[fixed((blocks, span, width)), fixed((shards, cols * width // shards // LANES, LANES)), fixed((width, LANES)), fixed(residual.shape), ANY],
            scratch_shapes=[
                pltpu.SemaphoreType.DMA((2,)),
                pltpu.VMEM((2, total, LANES), jnp.bfloat16),
                pltpu.VMEM((2, total, LANES), jnp.bfloat16),
                pltpu.VMEM((HEAD, total), jnp.bfloat16),
                pltpu.VMEM((total, LANES), jnp.float32),
                pltpu.VMEM((total, LANES), jnp.float32),
                pltpu.VMEM((blocks, span, LANES), jnp.float32),
                pltpu.VMEM((LANES, span), jnp.float32),
                pltpu.VMEM((cols, width), jnp.float32),
                pltpu.VMEM(w_out.shape, jnp.float32),
                pltpu.VMEM((2, total, span), jnp.bfloat16),
                pltpu.VMEM((2, total, span), jnp.bfloat16),
            ]
            + Collect.boxes(shards, *residual.shape)
            + GridSum.scratch(reps, 2 * len(experts), grad_gate_up.shape[1] // 2, grad_gate_up.shape[2]),
        ),
        out_shape=[
            shape((blocks, span, width), jnp.bfloat16),
            shape((shards, cols * width // shards // LANES, LANES), jnp.bfloat16),
            shape((width, LANES), jnp.bfloat16),
            shape(residual.shape, jnp.bfloat16),
            shape(grad_gate_up.shape, jnp.bfloat16),
        ],
        input_output_aliases={13: 4},
        compiler_params=remote_params(5, 60),
        cost_estimate=cost(34),
        name="attend_backward",
    )(d_attn, q, kv, mix, lse, start, w_out, w, cut(first), cut(cosine), cut(sine), o_parts, residual, grad_gate_up, head_sum)


MESH = pl.DeviceIdType.MESH


def chip_spot():
    me = lax.axis_index("shard")
    return me, me // 2, me % 2


def greet(others):
    barrier = pltpu.get_barrier_semaphore()
    for other in others:
        pl.semaphore_signal(barrier, inc=1, device_id=other, device_id_type=MESH)
    pl.semaphore_wait(barrier, len(others))


def greet_shard(shards):
    me = lax.axis_index("shard")
    greet([{"shard": lax.rem(me + k, shards)} for k in range(1, shards)])


def remote(src, dst, send_sem, recv_sem, target):
    return pltpu.make_async_remote_copy(
        src_ref=src,
        dst_ref=dst,
        send_sem=send_sem,
        recv_sem=recv_sem,
        device_id=target,
        device_id_type=MESH,
    )


def halves(rows):
    first = rows // 32 * 16
    return [(0, first), (first, rows - first)]


class Spread:
    def __init__(self, chips, src, out, sems):
        self.chips, self.src, self.out = chips, src, out
        self.own_sem, self.right_sem, self.left_sem, self.cross_sem, self.recv_sem = sems
        self.me, self.chip, self.core = chip_spot()
        self.cuts = halves(out.shape[1])
        self.has_right, self.has_left = self.chip < chips - 1, self.chip > 0

    @staticmethod
    def sems(shards):
        dma = pltpu.SemaphoreType.DMA
        return [dma((2,)), dma((shards,)), dma((shards,)), dma((shards,)), dma((2 * shards,))]

    def copy(self, way, source, cut, from_src=False, core=None):
        block = 2 * source + (self.core if core is None else core)
        here = pl.ds(*self.cuts[cut])
        sem = dict(right=self.right_sem, left=self.left_sem, cross=self.cross_sem)[way].at[2 * source + cut]
        target = dict(right=self.me + 2, left=self.me - 2, cross=2 * self.chip + 1 - self.core)[way]
        held = self.src.at[here] if from_src else self.out.at[block, here]
        return remote(held, self.out.at[block, here], sem, self.recv_sem.at[2 * block + cut], {"shard": target})

    def own(self, cut):
        here = pl.ds(*self.cuts[cut])
        return pltpu.make_async_copy(self.src.at[here], self.out.at[self.me, here], self.own_sem.at[cut])

    def start(self, cut):
        pl.when(self.has_right)(lambda: self.copy("right", self.chip, cut, True).start())
        pl.when(self.has_left)(lambda: self.copy("left", self.chip, cut, True).start())
        self.copy("cross", self.chip, cut, True).start()
        self.own(cut).start()

    def each(self, action, tick=lambda: None):
        for hop in range(1, self.chips):
            for cut in range(2):
                for side in (-1, 1):
                    source = self.chip + side * hop
                    inside = (source >= 0) if side < 0 else (source < self.chips)
                    pl.when(inside)(functools.partial(action, source, side, cut))
                    tick()

    def carry(self, tick=lambda: None):
        def pass_on(source, side, cut):
            self.copy("cross", source, cut).wait_recv()
            if side < 0:
                pl.when(self.has_right)(lambda: self.copy("right", source, cut).start())
            else:
                pl.when(self.has_left)(lambda: self.copy("left", source, cut).start())
            self.copy("cross", source, cut).start()

        self.each(pass_on, tick)

    def settle(self):
        for source in range(self.chips):
            for cut in range(2):
                self.copy("cross", source, cut, core=1 - self.core).wait_recv()
        for cut in range(2):
            self.own(cut).wait()
            self.copy("cross", self.chip, cut, True).wait_send()
            pl.when(self.has_right)(lambda cut=cut: self.copy("right", self.chip, cut, True).wait_send())
            pl.when(self.has_left)(lambda cut=cut: self.copy("left", self.chip, cut, True).wait_send())

        def sent(source, side, cut):
            if side < 0:
                pl.when(self.has_right)(lambda: self.copy("right", source, cut).wait_send())
            else:
                pl.when(self.has_left)(lambda: self.copy("left", source, cut).wait_send())
            self.copy("cross", source, cut).wait_send()

        self.each(sent)


STRIP = 16


class Collect:
    def __init__(self, chips, parts, boxes):
        self.chips, self.parts = chips, parts
        self.mine, self.cross, self.inbox = boxes[:3]
        self.mine_sem, self.swap_send, self.swap_recv, self.on_send, self.right_recv, self.left_recv = boxes[3:]
        self.me, self.chip, self.core = chip_spot()
        self.cuts = halves(parts.shape[1])

    @staticmethod
    def boxes(shards, rows, width):
        chips = shards // 2
        box = lambda count: pltpu.VMEM((count, rows, width), jnp.bfloat16)
        dma = pltpu.SemaphoreType.DMA
        return [box(chips), box(chips), box(chips + 1), dma((chips,))] + [dma((shards,))] * 5

    def load(self, dest):
        return pltpu.make_async_copy(self.parts.at[2 * dest + self.core], self.mine.at[dest], self.mine_sem.at[dest])

    def swap(self, dest, cut):
        here, sem = pl.ds(*self.cuts[cut]), 2 * dest + cut
        return remote(
            self.parts.at[2 * dest + 1 - self.core, here], self.cross.at[dest, here],
            self.swap_send.at[sem], self.swap_recv.at[sem], {"shard": 2 * self.chip + 1 - self.core},
        )

    def slot(self, dest, side, chip):
        return dest if side > 0 else jnp.where(dest == chip, self.chips, dest)

    def onward(self, dest, side, cut):
        here, at = pl.ds(*self.cuts[cut]), 2 * dest + cut
        slot = self.slot(dest, side, self.chip + side)
        sem, target = (self.right_recv, self.me + 2) if side > 0 else (self.left_recv, self.me - 2)
        return remote(
            self.cross.at[dest, here], self.inbox.at[slot, here], self.on_send.at[at], sem.at[at], {"shard": target}
        )

    def arrived(self, dest, side, cut):
        here, at = pl.ds(*self.cuts[cut]), 2 * dest + cut
        box = self.inbox.at[self.slot(dest, side, self.chip)]
        sem = self.right_recv if side > 0 else self.left_recv
        remote(box.at[here], box.at[here], self.on_send.at[at], sem.at[at], {"shard": 2 * self.chip + 1 - self.core}).wait_recv()
        return box

    def each(self, action, hops=None, tick=lambda: None):
        for hop in range(self.chips - 1, 0, -1) if hops is None else hops:
            for cut in range(2):
                for side in (1, -1):
                    dest = self.chip + side * hop
                    inside = (dest < self.chips) if side > 0 else (dest >= 0)
                    pl.when(inside)(functools.partial(action, dest, side, cut))
                    tick()

    def start(self):
        def begin(dest, side, cut):
            self.swap(dest, cut).start()
            if cut == 0:
                self.load(dest).start()

        self.each(begin)
        for cut in range(2):
            self.swap(self.chip, cut).start()
        self.load(self.chip).start()

    def strips(self, cut, parts, store):
        base, size = self.cuts[cut]

        def body(i, c):
            here = pl.ds(pl.multiple_of(base + i * STRIP, STRIP), STRIP)
            total = parts[0][here].astype(jnp.float32)
            for part in parts[1:]:
                total = total + part[here].astype(jnp.float32)
            store(here, total)
            return c

        lax.fori_loop(0, size // STRIP, body, 0)

    def carry(self, hops=None, tick=lambda: None):
        def pass_on(dest, side, cut):
            if cut == 0:
                self.load(dest).wait()
            self.swap(dest, cut).wait_recv()
            inner = (self.chip > 0) if side > 0 else (self.chip < self.chips - 1)
            near = (self.mine.at[dest], self.cross.at[dest])

            def keep(here, total):
                self.cross[dest, here] = total.astype(jnp.bfloat16)

            pl.when(inner)(lambda: self.strips(cut, near + (self.arrived(dest, side, cut),), keep))
            pl.when(jnp.logical_not(inner))(lambda: self.strips(cut, near, keep))
            self.onward(dest, side, cut).start()

        self.each(pass_on, hops, tick)

    def finish(self, cut, store):
        chip = self.chip
        if cut == 0:
            self.load(chip).wait()
        self.swap(chip, cut).wait_recv()
        near = (self.mine.at[chip], self.cross.at[chip])

        @pl.when((chip > 0) & (chip < self.chips - 1))
        def _():
            both = (self.arrived(chip, 1, cut), self.arrived(chip, -1, cut))
            self.strips(cut, near + both, store)

        pl.when(chip == 0)(lambda: self.strips(cut, near + (self.arrived(chip, -1, cut),), store))
        pl.when(chip == self.chips - 1)(lambda: self.strips(cut, near + (self.arrived(chip, 1, cut),), store))

    def settle(self):
        for cut in range(2):
            self.swap(self.chip, cut).wait_send()
        self.each(lambda dest, side, cut: self.swap(dest, cut).wait_send())
        self.each(lambda dest, side, cut: self.onward(dest, side, cut).wait_send())


class Direct:
    def __init__(self, shards, src, out, send_sem, recv_sem):
        self.shards, self.src, self.out, self.send_sem, self.recv_sem = shards, src, out, send_sem, recv_sem
        self.me = lax.axis_index("shard")

    @staticmethod
    def sems(shards):
        return [pltpu.SemaphoreType.DMA((shards,)), pltpu.SemaphoreType.DMA((shards,))]

    def copy(self, k):
        target = lax.rem(self.me + k, self.shards)
        return remote(
            self.src(target), self.out(self.me), self.send_sem.at[k], self.recv_sem.at[self.me], {"shard": target}
        )

    def own(self):
        return pltpu.make_async_copy(self.src(self.me), self.out(self.me), self.send_sem.at[0])

    def start(self):
        self.own().start()
        for k in range(1, self.shards):
            self.copy(k).start()

    def settle(self):
        self.own().wait()
        for k in range(1, self.shards):
            source = lax.rem(self.me + k, self.shards)
            block = self.out(source)
            remote(block, block, self.send_sem.at[k], self.recv_sem.at[source], {"shard": source}).wait_recv()
        for k in range(1, self.shards):
            self.copy(k).wait_send()


ANY = pl.BlockSpec(memory_space=pl.ANY)
INNER = pl.BlockSpec(memory_space=pltpu.VMEM)


def remote_params(call, megabytes):
    return pltpu.CompilerParams(collective_id=call, has_side_effects=True, vmem_limit_bytes=megabytes << 20)


def cost(micros):
    return pl.CostEstimate(flops=0, bytes_accessed=int(micros * 3.2e6), transcendentals=0)


def open_kernel(shards, x_ref, small_ref, choice_ref, piece_ref, all_x, all_small, all_choice, all_piece, *sems):
    greet_shard(shards)
    spread = Spread(shards // 2, x_ref, all_x, sems[:5])
    for cut in range(2):
        spread.start(cut)
    direct = [
        Direct(shards, lambda target: piece_ref.at[target], lambda source: all_piece.at[source], *sems[5:7]),
        Direct(shards, lambda target: small_ref, lambda source: all_small.at[source], *sems[7:9]),
        Direct(shards, lambda target: choice_ref, lambda source: all_choice.at[source], *sems[9:11]),
    ]
    for one in direct:
        one.start()
    spread.carry()
    for one in direct:
        one.settle()
    spread.settle()


def open_gathers(x, small, choice, pieces, shards):
    wide = lambda a: jax.ShapeDtypeStruct((shards,) + a.shape, a.dtype)
    return pl.pallas_call(
        functools.partial(open_kernel, shards),
        out_shape=[wide(x), wide(small), wide(choice), jax.ShapeDtypeStruct(pieces.shape, pieces.dtype)],
        in_specs=[ANY] * 4,
        out_specs=[ANY] * 4,
        scratch_shapes=Spread.sems(shards) + Direct.sems(shards) * 3,
        compiler_params=remote_params(1, 60),
        cost_estimate=cost(45),
        name="open_gathers",
    )(x, small, choice, pieces)


def expert_ids(shape, per_row):
    row = lax.broadcasted_iota(jnp.int32, shape, 0)
    rows = EXPERTS // per_row
    return per_row * (row % rows) + row // rows


def gate_columns(logits, choice, ids):
    named = jnp.zeros(logits.shape, jnp.float32)
    for k in range(choice.shape[0]):
        named = jnp.where(choice[k : k + 1] == ids, 1.0, named)
    masked = jnp.where(named > 0, logits, NEG)
    weight = jnp.where(named > 0, jnp.exp(masked - jnp.max(masked, axis=0, keepdims=True)), 0.0)
    return weight / jnp.sum(weight, axis=0, keepdims=True)


def middle_kernel(
    shards, parts_ref, x_ref, gain_ref, router_ref, choice_ref, residual_ref, second_ref, gates_ref, all_ref, *scratch
):
    greet_shard(shards)
    chips = shards // 2
    collect = Collect(chips, parts_ref, scratch[:9])
    spread = Spread(chips, second_ref, all_ref, scratch[9:14])
    collect.start()
    collect.carry()
    for cut in range(2):

        def store(here, total):
            residual = x_ref[here].astype(jnp.float32) + total
            residual_ref[here] = residual
            inv = lax.rsqrt(jnp.mean(residual * residual, axis=1, keepdims=True) + EPSILON)
            second_ref[here] = (residual * inv * gain_ref[...]).astype(jnp.bfloat16)

        collect.finish(cut, store)
        spread.start(cut)
    logits = nt_dot(router_ref[...], second_ref[...])
    per_row = x_ref.shape[1] // x_ref.shape[0]
    gates_ref[...] = gate_columns(logits, choice_ref[...], expert_ids(logits.shape, per_row))
    spread.carry()
    collect.settle()
    spread.settle()


def middle(parts, x, gain, router_t, choice_t, shards):
    rows, width = x.shape
    shape = jax.ShapeDtypeStruct
    return pl.pallas_call(
        functools.partial(middle_kernel, shards),
        out_shape=[
            shape((rows, width), jnp.float32),
            shape((rows, width), jnp.bfloat16),
            shape((EXPERTS, rows), jnp.float32),
            shape((shards, rows, width), jnp.bfloat16),
        ],
        in_specs=[ANY] + [INNER] * 4,
        out_specs=[INNER] * 3 + [ANY],
        scratch_shapes=Collect.boxes(shards, rows, width) + Spread.sems(shards),
        compiler_params=remote_params(2, 60),
        cost_estimate=cost(75),
        name="middle",
    )(parts.reshape(shards, rows, width), x, gain, router_t, choice_t)


def turn_kernel(
    shards, reps, parts_ref, gd_in, residual_ref, cot_ref, gain_ref, gates_ref, second_ref, router_ref,
    dres_ref, dgain_ref, drouter_ref, all_ref, gd_ref, dsec_s, datt_s, *scratch
):
    me = lax.axis_index("shard")
    greet([{"shard": lax.rem(me + k, shards)} for k in range(1, shards)] + Exchange.partners(reps))
    chips = shards // 2
    rows, width = residual_ref.shape
    collect = Collect(chips, parts_ref, scratch[:9])
    spread = Spread(chips, datt_s, all_ref, scratch[9:14])
    sums = GridSum(reps, [(gd_ref.at[e], gd_ref.at[e]) for e in range(gd_ref.shape[0])], scratch[14:23])
    collect.start()
    sums.begin()
    tick, drain = pacer(sums.steps())
    collect.carry(tick=tick)

    def stash(here, total):
        dsec_s[here] = total

    for cut in range(2):
        collect.finish(cut, stash)
    lines = EXPERTS * rows // width
    d_gates = dsec_s[rows : rows + lines] + dsec_s[rows + lines : rows + 2 * lines]
    d_gates = jnp.concatenate([d_gates[:, k * rows : (k + 1) * rows] for k in range(width // rows)], axis=0)
    gates = gates_ref[...]
    d_logits = gates * (d_gates - jnp.sum(gates * d_gates, axis=0, keepdims=True))
    high = d_logits.astype(jnp.bfloat16)
    low = (d_logits - high.astype(jnp.float32)).astype(jnp.bfloat16)
    drouter_ref[...] = nn_dot(high, second_ref[...]) + nn_dot(low, second_ref[...])
    dgain_ref[...] = jnp.zeros_like(dgain_ref)
    high_t = jnp.transpose(high.astype(jnp.float32)).astype(jnp.bfloat16)
    low_t = jnp.transpose(low.astype(jnp.float32)).astype(jnp.bfloat16)
    for cut in range(2):
        half = rows // 2
        for k in range(2):
            here = slice(cut * half + k * half // 2, cut * half + (k + 1) * half // 2)
            d_second = dsec_s[here] + nn_dot(high_t[here], router_ref[...]) + nn_dot(low_t[here], router_ref[...])
            residual = residual_ref[here]
            inv = lax.rsqrt(jnp.mean(residual * residual, axis=1, keepdims=True) + EPSILON)
            normed = residual * inv
            dgain_ref[...] += jnp.sum(d_second * normed, axis=0, keepdims=True)
            d_norm = d_second * gain_ref[...]
            d_residual = cot_ref[here].astype(jnp.float32) + inv * (
                d_norm - normed * jnp.mean(d_norm * normed, axis=1, keepdims=True)
            )
            dres_ref[here] = d_residual
            datt_s[here] = d_residual.astype(jnp.bfloat16)
        spread.start(cut)
    spread.carry(tick)
    drain()
    collect.settle()
    spread.settle()


def turn(parts, grad_down, residual, cot, gain, gates, second, router_t, shards, reps):
    rows, width = residual.shape
    shape = jax.ShapeDtypeStruct
    return pl.pallas_call(
        functools.partial(turn_kernel, shards, reps),
        out_shape=[
            shape((rows, width), jnp.float32),
            shape((1, width), jnp.float32),
            shape((EXPERTS, width), jnp.float32),
            shape((shards, rows, width), jnp.bfloat16),
            shape(grad_down.shape, jnp.bfloat16),
        ],
        in_specs=[ANY] * 2 + [INNER] * 6,
        out_specs=[INNER] * 3 + [ANY] * 2,
        scratch_shapes=[
            pltpu.VMEM((parts.shape[1], width), jnp.float32),
            pltpu.VMEM((rows, width), jnp.bfloat16),
        ]
        + Collect.boxes(shards, parts.shape[1], width)
        + Spread.sems(shards)
        + GridSum.scratch(reps, grad_down.shape[0], grad_down.shape[1], width),
        input_output_aliases={1: 4},
        compiler_params=remote_params(3, 60),
        cost_estimate=cost(75),
        name="turn",
    )(parts, grad_down, residual, cot, gain, gates, second, router_t)


class Exchange:
    def __init__(self, reps, data, boxes, send_sem, recv_sem):
        self.data, self.boxes, self.send_sem, self.recv_sem = data, boxes, send_sem, recv_sem
        self.rep = lax.axis_index("rep")
        self.bits = reps.bit_length() - 1
        half = data.shape[0] // 2
        self.cuts = [(0, half), (half, half)]

    @staticmethod
    def scratch(reps, rows, dtype):
        bits = reps.bit_length() - 1
        dma = pltpu.SemaphoreType.DMA((2 * bits,))
        return [pltpu.VMEM((bits, rows, LANES), dtype), dma, dma]

    @staticmethod
    def partners(reps):
        rep = lax.axis_index("rep")
        bits = [1 << k for k in range(reps.bit_length() - 1)]
        return [{"rep": rep + bit - 2 * bit * ((rep // bit) % 2)} for bit in bits]

    def copy(self, stage, cut):
        here, sem = pl.ds(*self.cuts[cut]), 2 * stage + cut
        bit = 1 << (stage if cut == 0 else self.bits - 1 - stage)
        other = self.rep + bit - 2 * bit * ((self.rep // bit) % 2)
        return remote(
            self.data.at[here], self.boxes.at[stage, here], self.send_sem.at[sem], self.recv_sem.at[sem], {"rep": other}
        )

    def run(self, store):
        for cut in range(2):
            self.copy(0, cut).start()
        for stage in range(self.bits):
            for cut in range(2):
                copy = self.copy(stage, cut)
                copy.wait_recv()
                copy.wait_send()
                base, size = self.cuts[cut]
                strip = 64 if size % 64 == 0 else size

                def body(i, c):
                    here = pl.ds(pl.multiple_of(base + i * strip, 8), strip)
                    total = self.data[here].astype(jnp.float32) + self.boxes[stage, here].astype(jnp.float32)
                    if stage == self.bits - 1:
                        store(here, total)
                    else:
                        self.data[here] = total.astype(self.data.dtype)
                    return c

                lax.fori_loop(0, size // strip, body, 0)
                if stage < self.bits - 1:
                    self.copy(stage + 1, cut).start()


class GridSum:
    def __init__(self, reps, pieces, scratch):
        self.pieces, self.bits = pieces, reps.bit_length() - 1
        self.full, self.inbox, self.result = scratch[:3]
        self.load_sem, self.store_sem, self.down_send, self.down_recv, self.up_send, self.up_recv = scratch[3:]
        self.rep = lax.axis_index("rep")
        self.rows = self.full.shape[1]

    @staticmethod
    def scratch(reps, count, rows, width):
        count = max(count, 1)
        bits = reps.bit_length() - 1
        dma = pltpu.SemaphoreType.DMA
        return [
            pltpu.VMEM((count, rows, width), jnp.bfloat16),
            pltpu.VMEM((count, rows, width), jnp.bfloat16),
            pltpu.VMEM((count, rows, width), jnp.bfloat16),
            dma((count,)),
            dma((count,)),
        ] + [dma((count, bits))] * 4

    def spot(self, piece, stage):
        base, size = 0, self.rows
        bits = []
        for k in range(stage + 1):
            which = k if piece % 2 == 0 else self.bits - 1 - k
            bits.append((which, (self.rep // (1 << which)) % 2))
        for which, bit in bits[:-1]:
            size //= 2
            base = base + bit * size
        which, bit = bits[-1]
        size //= 2
        kept = pl.multiple_of(base + bit * size, size)
        given = pl.multiple_of(base + (1 - bit) * size, size)
        partner = self.rep + (1 << which) - 2 * (1 << which) * bit
        return kept, given, size, {"rep": partner}

    def box_at(self, stage):
        return sum(self.rows >> (k + 1) for k in range(stage))

    def down(self, piece, stage):
        kept, given, size, partner = self.spot(piece, stage)
        return remote(
            self.full.at[piece, pl.ds(given, size)], self.inbox.at[piece, pl.ds(self.box_at(stage), size)],
            self.down_send.at[piece, stage], self.down_recv.at[piece, stage], partner,
        )

    def up(self, piece, stage, given=False):
        kept, other, size, partner = self.spot(piece, stage)
        here = self.result.at[piece, pl.ds(other if given else kept, size)]
        return remote(here, here, self.up_send.at[piece, stage], self.up_recv.at[piece, stage], partner)

    def load(self, piece):
        return pltpu.make_async_copy(self.pieces[piece][0], self.full.at[piece], self.load_sem.at[piece])

    def store(self, piece):
        return pltpu.make_async_copy(self.result.at[piece], self.pieces[piece][1], self.store_sem.at[piece])

    def add(self, piece, stage):
        kept, given, size, partner = self.spot(piece, stage)
        strip = 32

        def body(i, c):
            here = pl.ds(pl.multiple_of(kept + i * strip, strip), strip)
            there = pl.ds(pl.multiple_of(self.box_at(stage) + i * strip, strip), strip)
            total = self.full[piece, here].astype(jnp.float32) + self.inbox[piece, there].astype(jnp.float32)
            held = self.result if stage == self.bits - 1 else self.full
            held[piece, here] = total.astype(jnp.bfloat16)
            return c

        lax.fori_loop(0, size // strip, body, 0)

    def begin(self):
        loaded = [piece for piece in range(len(self.pieces)) if self.pieces[piece][0] is not None]
        for piece in loaded:
            self.load(piece).start()
        for piece in range(len(self.pieces)):
            if piece in loaded:
                self.load(piece).wait()
            self.down(piece, 0).start()

    def sink(self, stage, piece):
        self.down(piece, stage).wait_recv()
        self.add(piece, stage)
        (self.down(piece, stage + 1) if stage < self.bits - 1 else self.up(piece, stage)).start()

    def rise(self, stage, piece):
        self.up(piece, stage, True).wait_recv()
        (self.up(piece, stage - 1) if stage else self.store(piece)).start()

    def settle(self):
        for piece in range(len(self.pieces)):
            for stage in range(self.bits):
                self.down(piece, stage).wait_send()
                self.up(piece, stage).wait_send()
            self.store(piece).wait()

    def steps(self):
        order = [functools.partial(self.sink, k, p) for k in range(self.bits) for p in range(len(self.pieces))]
        back = range(self.bits - 1, -1, -1)
        order += [functools.partial(self.rise, k, p) for k in back for p in range(len(self.pieces))]
        return order + [self.settle]


def pacer(steps):
    left = iter(steps)

    def tick(count=1):
        for unused in range(count):
            next(left, lambda: None)()

    def drain():
        for step in left:
            step()

    return tick, drain


def gate_up_pieces(ref, experts):
    half = ref.shape[1] // 2
    spots = [ref.at[e, pl.ds(k * half, half)] for e in experts for k in range(2)]
    return [(spot, spot) for spot in spots]


MINI = 48


def close_kernel(
    shards, reps, experts, dparts_ref, gu_in, x_ref, dres_ref, gain_ref, head_ref, outg_ref, drouter_ref,
    dgain_ref, dtok_ref, share_ref, small_ref, gu_ref, bulk_s, mini_s, sum_s, minis_s, *scratch
):
    me = lax.axis_index("shard")
    greet([{"shard": lax.rem(me + k, shards)} for k in range(1, shards)] + Exchange.partners(reps))
    chips = shards // 2
    tok = Collect(chips, dparts_ref, scratch[:9])
    piece = head_ref.shape[1]
    bulk_at = lambda source: bulk_s.at[pl.ds(pl.multiple_of(source * piece, piece), piece)]
    heads = Direct(shards, lambda target: head_ref.at[target], bulk_at, *scratch[9:11])
    mini = Direct(shards, lambda target: mini_s.at[target], lambda source: minis_s.at[source], *scratch[11:13])
    bulk_sum = Exchange(reps, bulk_s, *scratch[13:16])
    mini_sum = Exchange(reps, sum_s, *scratch[16:19])
    sums = GridSum(reps, gate_up_pieces(gu_ref, experts), scratch[19:28])
    tok.start()
    sums.begin()
    heads.start()
    tick, drain = pacer(sums.steps())
    bulk_s[shards * piece :] = outg_ref[...]
    cols = gain_ref.shape[1] // shards
    mini_s[...] = jnp.zeros_like(mini_s)
    for k in range(shards):
        here = slice(k * cols, (k + 1) * cols)
        mini_s[k, :EXPERTS, :cols] = drouter_ref[:, here]
        mini_s[k, EXPERTS : EXPERTS + 1, :cols] = dgain_ref[:, here]
    tok.carry(tick=tick)

    def finish_tok(here, d_first):
        x = x_ref[here].astype(jnp.float32)
        inv = lax.rsqrt(jnp.mean(x * x, axis=1, keepdims=True) + EPSILON)
        normed = x * inv
        term = jnp.sum(d_first * normed, axis=0, keepdims=True)
        for k in range(shards):
            mini_s[k, EXPERTS + 1 : EXPERTS + 2, :cols] += term[:, k * cols : (k + 1) * cols]
        d_norm = d_first * gain_ref[...]
        dtok_ref[here] = dres_ref[here] + inv * (d_norm - normed * jnp.mean(d_norm * normed, axis=1, keepdims=True))

    for cut in range(2):
        tok.finish(cut, finish_tok)
    mini.start()
    heads.settle()

    def keep_bulk(here, total):
        share_ref[here] = total

    bulk_sum.run(keep_bulk)
    mini.settle()
    total = minis_s[0]
    for k in range(1, shards):
        total = total + minis_s[k]
    sum_s[...] = total

    def keep_mini(here, total):
        small_ref[here] = total

    mini_sum.run(keep_mini)
    drain()
    tok.settle()


def close(d_parts, grad_gate_up, experts, x, d_residual, gain, head_parts, out_grad, d_router, d_gain, shards, reps):
    rows, width = x.shape
    shape = jax.ShapeDtypeStruct
    piece = head_parts.shape[1]
    bulk = shards * piece + out_grad.shape[0]
    f32, bf16 = jnp.float32, jnp.bfloat16
    deep = lambda a: a.reshape(shards, rows, width)
    return pl.pallas_call(
        functools.partial(close_kernel, shards, reps, experts),
        out_shape=[
            shape((rows, width), f32),
            shape((bulk, LANES), f32),
            shape((MINI, LANES), f32),
            shape(grad_gate_up.shape, bf16),
        ],
        in_specs=[ANY] * 2 + [INNER] * 7,
        out_specs=[INNER] * 3 + [ANY],
        input_output_aliases={1: 3},
        scratch_shapes=[
            pltpu.VMEM((bulk, LANES), bf16),
            pltpu.VMEM((shards, MINI, LANES), f32),
            pltpu.VMEM((MINI, LANES), f32),
            pltpu.VMEM((shards, MINI, LANES), f32),
        ]
        + Collect.boxes(shards, rows, width)
        + Direct.sems(shards) * 2
        + Exchange.scratch(reps, bulk, bf16)
        + Exchange.scratch(reps, MINI, f32)
        + GridSum.scratch(reps, 2 * len(experts), grad_gate_up.shape[1] // 2, width),
        compiler_params=remote_params(4, 60),
        cost_estimate=cost(70),
        name="close",
    )(deep(d_parts), grad_gate_up, x, d_residual, gain, head_parts, out_grad, d_router, d_gain)


def tn_dot(a, b):
    return lax.dot_general(a, b, (((0,), (0,)), ((), ())), preferred_element_type=jnp.float32)


def slot_picks(choice, first_expert, local):
    rows = choice.shape[1]
    named = []
    for e in range(8):
        hit = jnp.zeros((1, rows), jnp.float32)
        if e < local:
            hit = jnp.max(jnp.where(choice == first_expert + e, 1.0, 0.0), axis=0, keepdims=True)
        named.append(hit)
    named = jnp.concatenate(named, axis=0)
    earlier = lax.broadcasted_iota(jnp.int32, (rows, rows), 0) < lax.broadcasted_iota(jnp.int32, (rows, rows), 1)
    rank = nn_dot(named.astype(jnp.bfloat16), jnp.where(earlier, 1.0, 0.0).astype(jnp.bfloat16))
    rank = jnp.where(named > 0, rank, -1.0)
    slot = lax.broadcasted_iota(jnp.int32, (CAP, rows), 0).astype(jnp.float32)
    return [jnp.where(rank[e : e + 1] == slot, 1.0, 0.0) for e in range(local)]


def pick_kernel(first_ref, x_ref, g_ref, choice_ref, router_ref, xs_ref, gs_ref, gate_ref):
    local = xs_ref.shape[0]
    rows = x_ref.shape[1]
    x, choice, first_expert = x_ref[0], choice_ref[0], first_ref[0]
    logits = nt_dot(router_ref[...], x)
    ids = expert_ids(logits.shape, x.shape[1] // x.shape[0])
    gates = gate_columns(logits, choice, ids)
    picks = slot_picks(choice, first_expert, local)
    for e in range(local):
        own = jnp.sum(jnp.where(ids == first_expert + e, gates, 0.0), axis=0, keepdims=True)
        gate_ref[e, 0] = jnp.sum(picks[e] * own, axis=1, keepdims=True)
    pick = jnp.concatenate(picks, axis=0).astype(jnp.bfloat16)
    xs = nn_dot(pick, x).astype(jnp.bfloat16)
    gs = nn_dot(pick, g_ref[0]).astype(jnp.bfloat16)
    for e in range(local):
        xs_ref[e, 0] = xs[e * CAP : (e + 1) * CAP]
        gs_ref[e, 0] = gs[e * CAP : (e + 1) * CAP]


def expert_kernel(
    reps, experts, xs_ref, gs_ref, gate_ref, wgu_ref, wd_ref, y_ref, dy_ref, dgate_ref, ggu_ref, gd_ref, head_ref,
    hid_s, dg_s, dgu_s, *scratch
):
    expert = pl.program_id(0)
    slots = xs_ref.shape[1]
    chunk = 256
    sums = GridSum(reps, [(None, head_ref.at[k]) for k in range(2)], scratch)
    steps = sums.steps()
    pl.when(expert == 0)(lambda: greet(Exchange.partners(reps)))
    last = pl.num_programs(0) - 1

    def progress(when, steps):
        def some():
            for step in steps:
                step()

        pl.when(when)(some)

    def part(i, c):
        here = pl.ds(pl.multiple_of(i * chunk, chunk), chunk)
        gate = gate_ref[0, here]
        gate_up = nn_dot(xs_ref[0, here], wgu_ref[0])
        gate_part, up_part = gate_up[:, :FF], gate_up[:, FF:]
        sig = 1.0 / (1.0 + jnp.exp(-gate_part))
        silu = gate_part * sig
        hidden = (silu * up_part).astype(jnp.bfloat16)
        hid_s[here] = hidden
        out = nn_dot(hidden, wd_ref[0])
        g = gs_ref[0, here].astype(jnp.float32)
        dgate_ref[0, here] = jnp.sum(out * g, axis=1, keepdims=True)
        y_ref[0, here] = (out * gate).astype(jnp.bfloat16)
        d_out = (g * gate).astype(jnp.bfloat16)
        dg_s[here] = d_out
        d_hidden = nt_dot(d_out, wd_ref[0])
        d_up = (d_hidden * silu).astype(jnp.bfloat16)
        d_gate = (d_hidden * up_part * (sig * (1.0 + gate_part * (1.0 - sig)))).astype(jnp.bfloat16)
        dgu = jnp.concatenate([d_gate, d_up], axis=1)
        dgu_s[here] = dgu
        dy_ref[0, here] = nt_dot(dgu, wgu_ref[0]).astype(jnp.bfloat16)
        return c

    lax.fori_loop(0, slots // chunk, part, 0)
    done = 0
    if experts >= 4:
        progress(expert == 2, steps[2:4])
        progress(expert == 3, steps[4:6])
        done = 6
    cols = 256
    for k in range(xs_ref.shape[2] // cols):
        here = slice(k * cols, (k + 1) * cols)
        ggu_ref[0, here, :] = tn_dot(xs_ref[0, :, here], dgu_s[...]).astype(jnp.bfloat16)

    @pl.when(expert == 0)
    def _():
        half = ggu_ref.shape[1] // 2
        for k in range(2):
            sums.full[k] = ggu_ref[0, k * half : (k + 1) * half]
        sums.begin()

    for k in range(hid_s.shape[1] // cols):
        here = slice(k * cols, (k + 1) * cols)
        gd_ref[0, here, :] = tn_dot(hid_s[:, here], dg_s[...]).astype(jnp.bfloat16)

    if done:
        progress(expert == 1, steps[:2])
    progress(expert == last, steps[done:])


def combine_kernel(first_ref, choice_ref, y_ref, dy_ref, dgate_ref, out_ref, dout_ref):
    local = y_ref.shape[0]
    rows, width = out_ref.shape[1:]
    first_expert = first_ref[0]
    picks = slot_picks(choice_ref[0], first_expert, local)
    per_row = width // rows
    lines = EXPERTS // per_row
    line = lax.broadcasted_iota(jnp.int32, (lines, rows), 0)
    spots = [jnp.zeros((lines, rows), jnp.float32)] * per_row
    for e in range(local):
        d_gate = jnp.sum(picks[e] * dgate_ref[e, 0], axis=0, keepdims=True)
        for k in range(per_row):
            spots[k] = jnp.where(line * per_row + k == first_expert + e, d_gate, spots[k])
    d_gates = jnp.concatenate(spots, axis=1)
    high = d_gates.astype(jnp.bfloat16)
    low = (d_gates - high.astype(jnp.float32)).astype(jnp.bfloat16)
    dout_ref[0, rows:] = jnp.concatenate([high.astype(jnp.float32), low.astype(jnp.float32)], axis=0).astype(jnp.bfloat16)
    pick = jnp.concatenate(picks, axis=0).astype(jnp.bfloat16)
    out_ref[0] = tn_dot(pick, y_ref[:, 0].reshape(local * CAP, -1)).astype(jnp.bfloat16)
    dout_ref[0, :rows] = tn_dot(pick, dy_ref[:, 0].reshape(local * CAP, -1)).astype(jnp.bfloat16)


def run_experts(group_in, group_cot, group_choice, router_t, w_gate_up, w_down, first_expert, reps):
    shards, rows, width = group_in.shape
    local = w_down.shape[0]
    slots = shards * CAP
    shape = jax.ShapeDtypeStruct
    params = lambda mb: pltpu.CompilerParams(dimension_semantics=("arbitrary",), vmem_limit_bytes=mb << 20)
    source = pl.BlockSpec((1, rows, width), lambda n, first: (n, 0, 0))
    named = pl.BlockSpec((1, TOPK, rows), lambda n, first: (n, 0, 0))
    placed = pl.BlockSpec((local, 1, CAP, width), lambda n, first: (0, n, 0, 0))
    thin = pl.BlockSpec((local, 1, CAP, 1), lambda n, first: (0, n, 0, 0))
    bf16, f32 = jnp.bfloat16, jnp.float32
    xs, gs, gates = pl.pallas_call(
        pick_kernel,
        grid_spec=pltpu.PrefetchScalarGridSpec(
            num_scalar_prefetch=1,
            grid=(shards,),
            in_specs=[source, source, named, pl.BlockSpec(router_t.shape, lambda n, first: (0, 0))],
            out_specs=[placed, placed, thin],
        ),
        out_shape=[
            shape((local, shards, CAP, width), bf16),
            shape((local, shards, CAP, width), bf16),
            shape((local, shards, CAP, 1), f32),
        ],
        compiler_params=params(60),
        cost_estimate=cost(8),
        name="pick_rows",
    )(first_expert, group_in, group_cot, group_choice, router_t)
    flat = lambda a: a.reshape(local, slots, a.shape[3])
    each = lambda r, c: pl.BlockSpec((1, r, c), lambda e: (e, 0, 0))
    y, dy, dgate, ggu, gd, head = pl.pallas_call(
        functools.partial(expert_kernel, reps, local),
        grid=(local,),
        in_specs=[each(slots, width), each(slots, width), each(slots, 1), each(width, 2 * FF), each(FF, width)],
        out_specs=[each(slots, width), each(slots, width), each(slots, 1), each(width, 2 * FF), each(FF, width), ANY],
        out_shape=[
            shape((local, slots, width), bf16),
            shape((local, slots, width), bf16),
            shape((local, slots, 1), f32),
            shape(w_gate_up.shape, bf16),
            shape(w_down.shape, bf16),
            shape((2, width // 2, 2 * FF), bf16),
        ],
        scratch_shapes=[
            pltpu.VMEM((slots, FF), bf16),
            pltpu.VMEM((slots, width), bf16),
            pltpu.VMEM((slots, 2 * FF), bf16),
        ]
        + GridSum.scratch(reps, 2, width // 2, 2 * FF),
        compiler_params=remote_params(6, 60),
        cost_estimate=cost(42),
        name="experts",
    )(flat(xs), flat(gs), flat(gates), w_gate_up, w_down)
    deep = lambda a: a.reshape(local, shards, CAP, a.shape[2])
    extra = 2 * EXPERTS * rows // width
    out, d_out = pl.pallas_call(
        combine_kernel,
        grid_spec=pltpu.PrefetchScalarGridSpec(
            num_scalar_prefetch=1,
            grid=(shards,),
            in_specs=[named, placed, placed, thin],
            out_specs=[source, pl.BlockSpec((1, rows + extra, width), lambda n, first: (n, 0, 0))],
        ),
        out_shape=[
            shape((shards, rows, width), bf16),
            shape((shards, rows + extra, width), bf16),
        ],
        compiler_params=params(60),
        cost_estimate=cost(9),
        name="combine_rows",
    )(first_expert, group_choice, deep(y), deep(dy), deep(dgate))
    return out, d_out, ggu, gd, head


def layout(lengths, tok_index, prompt_len):
    order = jnp.arange(lengths.shape[0])
    starts = prompt_len + jnp.sum(jnp.where(order[None, :] < order[:, None], lengths[None, :], 0), axis=1)
    passed = tok_index[:, None] >= starts[None, :]
    seg_start = jnp.max(jnp.where(passed, starts[None, :], 0), axis=1)
    position = jnp.where(seg_start > 0, tok_index - seg_start + prompt_len, tok_index)
    return (seg_start, position)


def head_pieces(w_qkv, shards):
    rows = w_qkv.shape[0]
    query_width, key_width = HEADS * HEAD, KV_HEADS * HEAD
    part = w_qkv[:, :query_width].reshape(rows, shards, query_width // shards)
    part = jnp.pad(part, ((0, 0), (0, 0), (0, LANES - part.shape[2])))
    share = shards // KV_HEADS
    keys = jnp.repeat(
        w_qkv[:, query_width : query_width + key_width].reshape(rows, KV_HEADS, HEAD), share, axis=1
    )
    vals = jnp.repeat(w_qkv[:, query_width + key_width :].reshape(rows, KV_HEADS, HEAD), share, axis=1)
    return jnp.concatenate([part, keys, vals], axis=2).transpose(1, 0, 2)


def joined_heads(pieces, shards):
    rows = pieces.shape[2]
    query_part = HEADS * HEAD // shards
    share = shards // KV_HEADS
    query = pieces[:, :query_part].reshape(HEADS * HEAD, rows)
    key = jnp.sum(pieces[:, LANES : LANES + HEAD].reshape(KV_HEADS, share, HEAD, rows), axis=1)
    val = jnp.sum(pieces[:, LANES + HEAD :].reshape(KV_HEADS, share, HEAD, rows), axis=1)
    joined = jnp.concatenate(
        [query, key.reshape(KV_HEADS * HEAD, rows), val.reshape(KV_HEADS * HEAD, rows)], axis=0
    )
    return joined.T


def on_device(
    tokens, choices, cont_lengths, norm_attn, w_qkv, w_out, norm_ffn, w_router, w_gate_up, w_down, cotangent
):
    row_count, model_width = tokens.shape
    shards, reps = lax.axis_size("shard"), lax.axis_size("rep")
    group_len = row_count * shards
    prompt_len = group_len // 2
    own_rows = norm_attn.shape[0]
    per_row = model_width // row_count
    router_part = w_router.T.reshape(EXPERTS // per_row, per_row, own_rows).transpose(1, 0, 2)
    small = jnp.concatenate(
        [router_part.reshape(EXPERTS, own_rows), norm_attn[None], norm_ffn[None], jnp.zeros((6, own_rows), jnp.bfloat16)],
        axis=0,
    )
    choice_t = choices.T
    group_tokens, group_small, group_choice, w_heads = open_gathers(
        tokens, small, choice_t, head_pieces(w_qkv, shards), shards
    )
    held_cot, group_tokens = lax.optimization_barrier((cotangent, group_tokens))
    group_cot = lax.all_gather(held_cot, "shard", axis=0, tiled=True)
    group_small = group_small.transpose(1, 0, 2).reshape(small.shape[0], model_width)
    router_t = group_small[:EXPERTS]
    gain_attn = group_small[EXPERTS : EXPERTS + 1].astype(jnp.float32)
    gain_ffn = group_small[EXPERTS + 1 : EXPERTS + 2].astype(jnp.float32)
    w_heads = w_heads.reshape(model_width, 2 * LANES)
    own_out = jnp.pad(w_out, ((0, LANES - w_out.shape[0]), (0, 0)))
    group_index = jnp.arange(group_len, dtype=jnp.int32)
    seg_start, position = layout(cont_lengths[0], group_index, prompt_len)
    lane = jnp.arange(LANES, dtype=jnp.int32)
    half = HEAD // 2
    freq_table = 10000.0 ** (-(lane % half).astype(jnp.float32) / half)
    angle = position.astype(jnp.float32)[:, None] * freq_table[None, :]
    cosine = jnp.cos(angle)
    sine = jnp.sin(angle) * jnp.where(lane % HEAD < half, -1.0, 1.0)[None, :]
    start_row = seg_start[None, :]
    cosine, sine, start_row = lax.optimization_barrier((cosine, sine, start_row))
    out_parts, group_first, queries, key_values, mixed_t, log_total = attend_forward(
        group_tokens.reshape(group_len, model_width), gain_attn, w_heads, cosine, sine, own_out, start_row
    )
    residual, second_in, gates, group_in = middle(out_parts, tokens, gain_ffn, router_t, choice_t, shards)
    out_terms, d_terms, grad_gate_up, grad_down, head_sum = run_experts(
        group_in, group_cot.reshape(group_in.shape), group_choice, router_t, w_gate_up, w_down,
        lax.axis_index("shard")[None] * w_down.shape[0], reps,
    )
    d_residual, d_gain, d_router, group_d_attn, grad_down = turn(
        d_terms, grad_down, residual, cotangent, gain_ffn, gates, second_in, router_t, shards, reps
    )
    early = (1,) if group_len <= 2048 else ()
    d_parts, head_parts, out_grad, output, grad_gate_up = attend_backward(
        group_d_attn.reshape(group_len, model_width), queries, key_values, mixed_t, log_total, start_row,
        own_out, w_heads, group_first, cosine, sine, out_terms, residual, grad_gate_up, early, head_sum, shards, reps,
    )
    d_tokens, share, small_sum, grad_gate_up = close(
        d_parts, grad_gate_up, tuple(range(1 + len(early), w_down.shape[0])), tokens, d_residual, gain_attn, head_parts, out_grad, d_router, d_gain, shards, reps
    )
    lines = head_parts.shape[1]
    head_grads = share[: shards * lines].reshape(shards, lines, LANES // own_rows, own_rows)
    head_grads = head_grads.transpose(0, 2, 1, 3).reshape(shards, 2 * LANES, own_rows)
    out_share = share[shards * lines :].reshape(model_width // LANES, LANES, LANES).transpose(1, 0, 2)
    router_share = small_sum[:EXPERTS, :own_rows].reshape(per_row, EXPERTS // per_row, own_rows).transpose(2, 1, 0)
    return (
        output,
        d_tokens,
        small_sum[EXPERTS + 1, :own_rows],
        joined_heads(head_grads, shards),
        out_share.reshape(LANES, model_width)[: w_out.shape[0]],
        small_sum[EXPERTS, :own_rows],
        router_share.reshape(own_rows, EXPERTS),
        grad_gate_up.astype(jnp.float32),
        grad_down.astype(jnp.float32),
    )


def solution(mesh):
    return jax.shard_map(
        on_device,
        mesh=mesh,
        in_specs=(
            P(("rep", "shard"), None),
            P(("rep", "shard"), None),
            P("rep", None),
            P("shard"),
            P("shard", None),
            P("shard", None),
            P("shard"),
            P("shard", None),
            P("shard", None, None),
            P("shard", None, None),
            P(("rep", "shard"), None),
        ),
        out_specs=(
            P(("rep", "shard"), None),
            P(("rep", "shard"), None),
            P("shard"),
            P("shard", None),
            P("shard", None),
            P("shard"),
            P("shard", None),
            P("shard", None, None),
            P("shard", None, None),
        ),
        check_vma=False,
    )
```
